128 devices in a mesh: store: 8 (over y, core), batch: 16 (over z, x).
Axes of the slice: x: 4, y: 4, z: 4, core: 2. Of those that a mesh axis runs over, the one named last changes fastest.
Arguments:
- features: bfloat16 [8, 128, 128, 512], P('store', 'batch'), may hold values from -6 to 6
- diag_blocks: bfloat16 [8, 128, 128, 128], P('store', 'batch'), may hold values from 0 to 0.015625
- coupling_blocks: bfloat16 [8, 128, 128, 128], P('store', 'batch'), may hold values from 0 to 0.0078125
- neighbour: int32 [8, 128], P('store', 'batch'), may hold values from 0 to 127, as said below
- assignment: int32 [8, 128], P('store', 'batch'), may hold values from 0 to 15, as said below
- feature_drop: int32 [8, 128, 2, 512], P('store', 'batch'), may hold values 0 or 1
- edge_drop: int32 [8, 128, 2, 128], P('store', 'batch'), may hold values 0 or 1
- weights: bfloat16 [2, 512, 512], replicated, may hold values from -0.25 to 0.25
Outputs:
- weight_grads: float32 [2, 512, 512], replicated
The draws below stay inside these ranges and needn't reach their ends.
Inputs may be any that keep to these rules, and one draw needn't show every extreme that they name: `assignment`: within a group, the 8 clusters of one device (consecutive indices) go to distinct batches; in every group some batch receives one cluster from every device. neighbour[g, c] is a cluster of the same group with the same assignment as c, possibly c itself.
All inputs are finite; a program needn't handle non-finite values. No bound on the sum of `feature_drop` or of `edge_drop` on one device may be relied on, other than what follows from the above.
Results may differ from the reference program's by a relative error of at most 0.0025.
Values may be sent and summed in bfloat16 or wider, within the bound.
No kernel may reach another device: no remote copies, remote signals or barrier semaphores. Data moves between devices by JAX's collectives and lax.ppermute only.
A program may use at most 128 MiB of HBM per device.

```python
import jax
import jax.numpy as jnp
from jax import lax

NODE_FEATURES = 512
R = 128
LAYERS = 2
CPD = 8
GROUPS = 8
CG = 128
N_BATCH = 16


def assignment_and_neighbour(key):
    key_busy = jax.random.fold_in(key, 101)
    key_dest = jax.random.fold_in(key, 202)
    key_order = jax.random.fold_in(key, 303)
    key_pair = jax.random.fold_in(key, 404)
    busiest = jax.random.randint(key_busy, (GROUPS,), 0, N_BATCH)
    dest_index = jnp.arange(N_BATCH, dtype=jnp.int32)
    dest_scores = jax.random.randint(key_dest, (GROUPS, N_BATCH, N_BATCH), 0, 1 << 20) * N_BATCH + dest_index[None, None, :]
    dest_scores = jnp.where(dest_index[None, None, :] == busiest[:, None, None], -1, dest_scores)
    ordered = jnp.argsort(dest_scores, axis=-1, stable=True).astype(jnp.int32)
    chosen = ordered[:, :, :CPD]
    slot_index = jnp.arange(CPD, dtype=jnp.int32)
    slot_scores = jax.random.randint(key_order, (GROUPS, N_BATCH, CPD), 0, 1 << 20) * CPD + slot_index[None, None, :]
    shuffle = jnp.argsort(slot_scores, axis=-1, stable=True)
    placed = jnp.take_along_axis(chosen, shuffle, axis=-1)
    assigned = placed.reshape(GROUPS, CG).astype(jnp.int32)
    cluster_index = jnp.arange(CG, dtype=jnp.int32)
    pair_scores = jax.random.randint(key_pair, (GROUPS, CG, CG), 0, 1 << 20) * CG + cluster_index[None, None, :]
    same_batch = assigned[:, :, None] == assigned[:, None, :]
    masked = jnp.where(same_batch, pair_scores, -1)
    partner_node = jnp.argmax(masked, axis=-1).astype(jnp.int32)
    return (assigned, partner_node)


def draw_assignment(key, part):
    return assignment_and_neighbour(key)[0]


def draw_neighbour(key, part):
    return assignment_and_neighbour(key)[1]


def touch_ends(values, own_key, smallest, top_value):
    shape = values.shape
    place = [jax.random.randint(jax.random.fold_in(own_key, axis), (), 0, shape[axis]) for axis in range(len(shape))]
    values = values.at[tuple(place)].set(smallest)
    longest = shape.index(max(shape))
    place[longest] = (place[longest] + 1) % shape[longest]
    return values.at[tuple(place)].set(top_value)


def levels(stream_key, shape, pieces, smallest, high):
    def one(dim, shards_of):
        heights = jax.random.uniform(jax.random.fold_in(jax.random.fold_in(stream_key, 6), dim), (shards_of,), jnp.float32, smallest / len(pieces), high / len(pieces))
        return jnp.repeat(jnp.exp(heights), shape[dim] // shards_of).reshape((-1,) + (1,) * (len(shape) - dim - 1))

    level = one(*pieces[0])
    for cut in pieces[1:]:
        level = level * one(*cut)
    return level


def centred(rng, extent, scale, limit, shards=(), kind=jnp.bfloat16):
    values = scale * jax.random.normal(rng, extent, jnp.float32)
    if shards:
        values = values * levels(rng, extent, shards, -0.22, 0.18)
    return jnp.clip(values, -limit, limit).astype(kind)


def setup_inputs(seed: int = 0) -> dict:
    splits = jax.random.split(jax.random.key(seed), 9)
    return {
        "features": centred(splits[0], (GROUPS, CG, R, NODE_FEATURES), 1.0, 6.0, ((0, 8), (1, 16))),
        "diag_blocks": jnp.clip(0.015625 * jax.random.uniform(splits[1], (GROUPS, CG, R, R), jnp.float32) ** levels(splits[1], (GROUPS, CG, R, R), ((0, 8), (1, 16)), -0.2, 0.2), 0.0, 0.015625).astype(jnp.bfloat16),
        "coupling_blocks": jnp.clip(0.0078125 * jax.random.uniform(splits[2], (GROUPS, CG, R, R), jnp.float32) ** levels(splits[2], (GROUPS, CG, R, R), ((0, 8), (1, 16)), -0.2, 0.2), 0.0, 0.0078125).astype(jnp.bfloat16),
        "neighbour": draw_neighbour(jax.random.fold_in(splits[8], 71), 0),
        "assignment": draw_assignment(jax.random.fold_in(splits[8], 71), 0),
        "feature_drop": touch_ends((jax.random.randint(splits[5], (GROUPS, CG, 2, NODE_FEATURES), 0, 4) < 3).astype(jnp.int32), jax.random.fold_in(splits[5], 1), 0, 1),
        "edge_drop": touch_ends((jax.random.randint(splits[6], (GROUPS, CG, 2, R), 0, 5) < 4).astype(jnp.int32), jax.random.fold_in(splits[6], 1), 0, 1),
        "weights": centred(splits[7], (LAYERS, NODE_FEATURES, NODE_FEATURES), NODE_FEATURES ** -0.5, 0.25),
    }


SOFTMAX_TEMPER = 0.5
EPSILON = 1e-05

def group_gradients(features, diag_blocks, coupling_blocks, neighbour, assignment, feature_drop, edge_drop, weights):
    view_keep = jnp.transpose(feature_drop, (1, 0, 2))[:, :, None, :].astype(jnp.bfloat16)
    edge_keep = jnp.transpose(edge_drop, (1, 0, 2))[:, :, :, None].astype(jnp.bfloat16)
    adjacency = diag_blocks.astype(jnp.float32)
    couplings = coupling_blocks.astype(jnp.float32)
    hidden = features[None] * view_keep
    stored_inputs = []
    stored_pre = []
    summed = None
    for layer_index in range(LAYERS):
        projected = jnp.einsum('vcxf,fg->vcxg', hidden.astype(jnp.float32), weights[layer_index].astype(jnp.float32)).astype(jnp.bfloat16)
        messages = projected * edge_keep
        borrowed = messages[:, neighbour]
        summed = jnp.einsum('cxy,vcyf->vcxf', adjacency, messages.astype(jnp.float32)) + jnp.einsum('cxy,vcyf->vcxf', couplings, borrowed.astype(jnp.float32))
        stored_inputs.append(hidden)
        stored_pre.append(summed)
        hidden = jnp.maximum(summed, 0.0).astype(jnp.bfloat16)
    pooled = lax.optimization_barrier(jnp.mean(jnp.maximum(summed, 0.0), axis=2))
    inv_norm = lax.rsqrt(lax.optimization_barrier(jnp.mean(pooled * pooled, axis=-1)) + EPSILON)
    unit_vecs = pooled * inv_norm[..., None]
    scale_factor = 1.0 / (NODE_FEATURES * SOFTMAX_TEMPER)
    scores = jnp.dot(unit_vecs[0], unit_vecs[1].T, precision=lax.Precision.HIGHEST) * scale_factor
    same_batch = (assignment[:, None] == assignment[None, :]).astype(jnp.float32)
    weighted = jnp.exp(scores) * same_batch
    coeffs = weighted / lax.optimization_barrier(jnp.sum(weighted, axis=1, keepdims=True)) - jnp.eye(CG, dtype=jnp.float32)
    unit_grad = jnp.stack([jnp.dot(coeffs, unit_vecs[1], precision=lax.Precision.HIGHEST), jnp.dot(coeffs.T, unit_vecs[0], precision=lax.Precision.HIGHEST)]) * scale_factor
    pooled_grad = inv_norm[..., None] * unit_grad - (inv_norm ** 3 * lax.optimization_barrier(jnp.sum(pooled * unit_grad, axis=-1)) / NODE_FEATURES)[..., None] * pooled
    pre_grad = (pooled_grad / R)[:, :, None, :] * (summed > 0).astype(jnp.float32)
    gradients = []
    for layer_index in reversed(range(LAYERS)):
        rounded = pre_grad.astype(jnp.bfloat16).astype(jnp.float32)
        spread = jnp.einsum('cxy,vcxf->vcyf', couplings, rounded)
        gathered = jax.ops.segment_sum(jnp.moveaxis(spread, 1, 0), neighbour, num_segments=CG)
        message_grad = jnp.einsum('cxy,vcxf->vcyf', adjacency, rounded) + jnp.moveaxis(gathered, 0, 1)
        proj_grad = (message_grad * edge_keep.astype(jnp.float32)).astype(jnp.bfloat16)
        gradients.append(jnp.einsum('vcxf,vcxg->fg', stored_inputs[layer_index].astype(jnp.float32), proj_grad.astype(jnp.float32)))
        if layer_index > 0:
            hidden_grad = jnp.einsum('vcxg,fg->vcxf', proj_grad.astype(jnp.float32), weights[layer_index].astype(jnp.float32))
            pre_grad = hidden_grad * (stored_pre[layer_index - 1] > 0).astype(jnp.float32)
    return jnp.stack(gradients[::-1])

def reference(features, diag_blocks, coupling_blocks, neighbour, assignment, feature_drop, edge_drop, weights):

    def one_group(items):
        return group_gradients(items[0], items[1], items[2], items[3], items[4], items[5], items[6], weights)
    per_group = lax.map(one_group, (features, diag_blocks, coupling_blocks, neighbour, assignment, feature_drop, edge_drop))
    return lax.optimization_barrier(jnp.sum(per_group, axis=0))
```

```python
import jax
import jax.numpy as jnp
from jax import lax
from jax.experimental import pallas as pl
from jax.experimental.pallas import tpu as pltpu
from jax.sharding import PartitionSpec as P

SOFTMAX_TEMPER = 0.5
EPSILON = 1e-05

LANES = 128
META = 16


def pack_kernel(
    assign, neighbour, features, diag, coupling, feature_drop, edge_drop, send, meta
):
    owned, nodes, columns = features.shape[1:]
    blocks = columns // LANES
    meta[...] = jnp.zeros_like(meta)
    for k in range(owned):
        target = assign[0, k]
        for j in range(blocks):
            send[target, pl.ds(j * nodes, nodes), :] = features[0, k, :, pl.ds(j * LANES, LANES)]
        send[target, pl.ds(blocks * nodes, nodes), :] = diag[0, k]
        send[target, pl.ds((blocks + 1) * nodes, nodes), :] = coupling[0, k]
        for v in range(2):
            for j in range(blocks):
                meta[target, v * blocks + j, :] = feature_drop[
                    0, k, v, pl.ds(j * LANES, LANES)
                ].astype(jnp.float32)
            meta[target, 2 * blocks + v, :] = edge_drop[0, k, v, :].astype(jnp.float32)
        slot = neighbour[0, k] // owned + 1
        meta[target, 2 * blocks + 2, :] = jnp.full((LANES,), slot, jnp.float32)
    send[:, pl.ds((blocks + 2) * nodes, META), :] = meta[...].astype(jnp.bfloat16)


def dot(a, b, contract, precision=None):
    return lax.dot_general(
        a, b, (contract, ((), ())), precision=precision, preferred_element_type=jnp.float32
    )


def step_kernel(
    core, weights, recv, out,
    rbuf, meta, slots, slot_ids, h0, p0, p1, h1, adj, active, acc, pooled,
    sems, meta_sem, slot_sem,
):
    count = recv.shape[0]
    columns = weights.shape[1]
    blocks = columns // LANES
    nodes = adj.shape[1]
    body = (blocks + 2) * nodes
    rows = 2 * nodes
    low = jnp.bfloat16

    meta_copy = pltpu.make_async_copy(recv.at[:, pl.ds(body, META), :], meta, meta_sem)
    meta_copy.start()
    for s in range(count):
        pltpu.make_async_copy(recv.at[s, pl.ds(0, body), :], rbuf.at[s], sems.at[s]).start()
    meta_copy.wait()
    slots[...] = meta[...].astype(jnp.float32)
    pooled[2, :, pl.ds(0, LANES)] = slots[:, 2 * blocks + 2, :]
    nbr = slots[:, 2 * blocks + 2, :].astype(jnp.int32) - 1
    own = lax.broadcasted_iota(jnp.int32, nbr.shape, 0)
    linked = jnp.where(nbr < 0, own, nbr)

    def put_ids(ids_vmem):
        ids_vmem[...] = linked
        copy = pltpu.make_async_copy(ids_vmem, slot_ids, slot_sem)
        copy.start()
        copy.wait()

    pl.run_scoped(put_ids, pltpu.VMEM((count, LANES), jnp.int32))

    def project(s, carry):
        pltpu.make_async_copy(recv.at[s, pl.ds(0, body), :], rbuf.at[s], sems.at[s]).wait()
        n = slot_ids[s, 0]
        own_rows = rbuf[s, pl.ds(0, blocks * nodes), :].reshape(blocks, nodes, LANES)
        diag = rbuf[s, pl.ds(blocks * nodes, nodes), :]
        coupling = rbuf[s, pl.ds((blocks + 1) * nodes, nodes), :]
        zero = jnp.zeros((), low)
        for v in range(2):
            pieces = []
            for j in range(blocks):
                keep = slots[s, pl.ds(v * blocks + j, 1), :] > 0.5
                pieces.append(jnp.where(keep, own_rows[j], zero))
            base = s * rows + v * nodes
            h0[pl.ds(base, nodes), :] = jnp.concatenate(pieces, axis=1)
            own_keep = slots[s, pl.ds(2 * blocks + v, 1), :] > 0.5
            far_keep = slots[n, pl.ds(2 * blocks + v, 1), :] > 0.5
            adj[2 * s + v] = jnp.concatenate(
                [jnp.where(own_keep, diag, zero), jnp.where(far_keep, coupling, zero)], axis=1
            )
        base = s * rows
        p0[pl.ds(base, rows), :] = dot(
            h0[pl.ds(base, rows), :], weights[0], ((1,), (0,))
        ).astype(low)
        acc[pl.ds(base, rows), :] = jnp.zeros((rows, columns), jnp.float32)
        return carry

    lax.fori_loop(0, count, project, 0)

    def gather(source, s, n, v):
        return dot(
            adj[2 * s + v],
            jnp.concatenate(
                [
                    source[pl.ds(s * rows + v * nodes, nodes), :],
                    source[pl.ds(n * rows + v * nodes, nodes), :],
                ],
                axis=0,
            ),
            ((1,), (0,)),
        )

    def first_layer(s, carry):
        n = slot_ids[s, 0]
        for v in range(2):
            h1[pl.ds(s * rows + v * nodes, nodes), :] = jnp.maximum(
                gather(p0, s, n, v), 0.0
            ).astype(low)
        p1[pl.ds(s * rows, rows), :] = dot(
            h1[pl.ds(s * rows, rows), :], weights[1], ((1,), (0,))
        ).astype(low)
        return carry

    lax.fori_loop(0, count, first_layer, 0)

    def second_layer(s, carry):
        n = slot_ids[s, 0]
        for v in range(2):
            summed = jnp.maximum(gather(p1, s, n, v), 0.0)
            active[pl.ds(s * rows + v * nodes, nodes), :] = jnp.where(
                summed > 0, 1.0, 0.0
            ).astype(low)
            pooled[v, pl.ds(s, 1), :] = jnp.sum(summed, axis=0, keepdims=True) * (1.0 / nodes)
        return carry

    lax.fori_loop(0, count, second_layer, 0)

    flags = jnp.where(pooled[2, :, pl.ds(0, LANES)] > 0.5, 1.0, 0.0)
    occ_col = flags[:, 0:1]
    occ_row = dot(
        jnp.full((8, LANES), 1.0 / LANES, jnp.float32), flags, ((1,), (1,)), lax.Precision.HIGHEST
    )[0:1, :]
    means = [pooled[0], pooled[1]]
    inv = [
        lax.rsqrt(jnp.mean(e * e, axis=-1, keepdims=True) + EPSILON) for e in means
    ]
    unit = [e * i for e, i in zip(means, inv)]
    scale = 1.0 / (columns * SOFTMAX_TEMPER)
    high = lax.Precision.HIGHEST
    scores = dot(unit[0], unit[1], ((1,), (1,)), high) * scale
    weighted = jnp.exp(scores) * occ_row
    totals = jnp.where(occ_col > 0.5, jnp.sum(weighted, axis=1, keepdims=True), 1.0)
    row_id = lax.broadcasted_iota(jnp.int32, (count, count), 0)
    col_id = lax.broadcasted_iota(jnp.int32, (count, count), 1)
    eye = jnp.where(row_id == col_id, 1.0, 0.0)
    coeffs = (weighted / totals - eye) * occ_col
    unit_grad = [
        dot(coeffs, unit[1], ((1,), (0,)), high) * scale,
        dot(coeffs, unit[0], ((0,), (0,)), high) * scale,
    ]
    for v in range(2):
        grad = (
            inv[v] * unit_grad[v]
            - (inv[v] ** 3 * jnp.sum(means[v] * unit_grad[v], axis=-1, keepdims=True) / columns)
            * means[v]
        )
        pooled[v] = (grad / nodes).astype(low).astype(jnp.float32)

    def scatter(s, v, grad):
        n = slot_ids[s, 0]
        spread = dot(adj[2 * s + v], grad, ((0,), (0,)))
        mine = pl.ds(s * rows + v * nodes, nodes)
        acc[mine, :] = acc[mine, :] + spread[:nodes]
        far = pl.ds(n * rows + v * nodes, nodes)
        acc[far, :] = acc[far, :] + spread[nodes:]

    def second_back(s, carry):
        for v in range(2):
            row = pooled[v, pl.ds(s, 1), :].astype(low)
            scatter(s, v, active[pl.ds(s * rows + v * nodes, nodes), :] * row)
        return carry

    lax.fori_loop(0, count, second_back, 0)

    keep_one = core[0] ^ 1
    keep_zero = core[0]
    chunk = 4 * rows
    out[...] = jnp.zeros_like(out)

    def second_weights(i, carry):
        span = pl.ds(i * chunk, chunk)
        grad = acc[span, :].astype(low)
        acc[span, :] = jnp.zeros((chunk, columns), jnp.float32)
        hidden = h1[span, :]
        out[keep_one] = out[keep_one] + dot(hidden, grad, ((0,), (0,)))
        below = dot(grad, weights[1], ((1,), (1,)))
        p0[span, :] = jnp.where(hidden > 0, below, 0.0).astype(low)
        return carry

    lax.fori_loop(0, count // 4, second_weights, 0)

    def first_back(s, carry):
        for v in range(2):
            scatter(s, v, p0[pl.ds(s * rows + v * nodes, nodes), :])
        return carry

    lax.fori_loop(0, count, first_back, 0)

    def first_weights(i, carry):
        span = pl.ds(i * chunk, chunk)
        out[keep_zero] = out[keep_zero] + dot(
            h0[span, :], acc[span, :].astype(low), ((0,), (0,))
        )
        return carry

    lax.fori_loop(0, count // 4, first_weights, 0)


def local(
    features, diag_blocks, coupling_blocks, neighbour, assignment, feature_drop, edge_drop, weights
):
    count = lax.axis_size("batch")
    stores = lax.axis_size("store")
    _, owned, nodes, columns = features.shape
    blocks = columns // LANES
    body = (blocks + 2) * nodes
    low = jnp.bfloat16
    smem = pl.BlockSpec(memory_space=pltpu.SMEM)
    vmem = pl.BlockSpec(memory_space=pltpu.VMEM)
    raw = pl.BlockSpec(memory_space=pl.ANY)
    send = pl.pallas_call(
        pack_kernel,
        out_shape=jax.ShapeDtypeStruct((count, body + META, LANES), low),
        in_specs=[smem, smem, vmem, vmem, vmem, vmem, vmem],
        out_specs=vmem,
        scratch_shapes=[pltpu.VMEM((count, META, LANES), jnp.float32)],
        name="pack",
    )(assignment, neighbour, features, diag_blocks, coupling_blocks, feature_drop, edge_drop)
    recv = lax.all_to_all(send, "batch", split_axis=0, concat_axis=0, tiled=True)
    parity = lax.axis_index("store") % 2
    total = count * 2 * nodes
    halves = pl.pallas_call(
        step_kernel,
        out_shape=jax.ShapeDtypeStruct((2, columns, columns), jnp.float32),
        in_specs=[smem, vmem, raw],
        out_specs=vmem,
        scratch_shapes=[
            pltpu.VMEM((count, body, LANES), low),
            pltpu.VMEM((count, META, LANES), low),
            pltpu.VMEM((count, META, LANES), jnp.float32),
            pltpu.SMEM((count, LANES), jnp.int32),
            pltpu.VMEM((total, columns), low),
            pltpu.VMEM((total, columns), low),
            pltpu.VMEM((total, columns), low),
            pltpu.VMEM((total, columns), low),
            pltpu.VMEM((2 * count, nodes, 2 * nodes), low),
            pltpu.VMEM((total, columns), low),
            pltpu.VMEM((total, columns), jnp.float32),
            pltpu.VMEM((3, count, columns), jnp.float32),
            pltpu.SemaphoreType.DMA((count,)),
            pltpu.SemaphoreType.DMA,
            pltpu.SemaphoreType.DMA,
        ],
        compiler_params=pltpu.CompilerParams(vmem_limit_bytes=56 << 20),
        name="step",
    )(parity.reshape(1).astype(jnp.int32), weights, recv)

    swap = [(s, s ^ 1) for s in range(stores)]
    kept = halves[0] + lax.ppermute(halves[1], "store", swap)
    chips = stores // 2 * count
    groups = [
        [s * count + b for s in range(c, stores, 2) for b in range(count)] for c in range(2)
    ]
    axes = ("store", "batch")
    pieces = lax.all_to_all(
        kept.reshape(chips, columns // chips, columns),
        axes, split_axis=0, concat_axis=0, axis_index_groups=groups, tiled=True,
    )
    piece = jnp.sum(pieces, axis=0).astype(low)
    layer = lax.all_to_all(
        jnp.broadcast_to(piece[None], (chips,) + piece.shape),
        axes, split_axis=0, concat_axis=0, axis_index_groups=groups, tiled=True,
    ).reshape(columns, columns)
    other = lax.ppermute(layer, "store", swap)
    first = parity == 0
    return jnp.stack(
        [jnp.where(first, layer, other), jnp.where(first, other, layer)]
    ).astype(jnp.float32)


def solution(mesh):
    return jax.shard_map(
        local,
        mesh=mesh,
        in_specs=(
            P("store", "batch", None, None),
            P("store", "batch", None, None),
            P("store", "batch", None, None),
            P("store", "batch"),
            P("store", "batch"),
            P("store", "batch", None, None),
            P("store", "batch", None, None),
            P(),
        ),
        out_specs=P(),
        check_vma=False,
    )
```

```python
import jax
import jax.numpy as jnp
from jax import lax
from jax.experimental import pallas as pl
from jax.experimental.pallas import tpu as pltpu
from jax.sharding import PartitionSpec as P

SOFTMAX_TEMPER = 0.5
EPSILON = 1e-05

LANES = 128
META = 16


def pack_kernel(
    assign, neighbour, features, diag, coupling, feature_drop, edge_drop, send, meta
):
    owned, nodes, columns = features.shape[1:]
    blocks = columns // LANES
    meta[...] = jnp.zeros_like(meta)
    for k in range(owned):
        target = assign[0, k]
        for j in range(blocks):
            send[target, pl.ds(j * nodes, nodes), :] = features[0, k, :, pl.ds(j * LANES, LANES)]
        send[target, pl.ds(blocks * nodes, nodes), :] = diag[0, k]
        send[target, pl.ds((blocks + 1) * nodes, nodes), :] = coupling[0, k]
        for v in range(2):
            for j in range(blocks):
                meta[target, v * blocks + j, :] = feature_drop[
                    0, k, v, pl.ds(j * LANES, LANES)
                ].astype(jnp.float32)
            meta[target, 2 * blocks + v, :] = edge_drop[0, k, v, :].astype(jnp.float32)
        slot = neighbour[0, k] // owned + 1
        meta[target, 2 * blocks + 2, :] = jnp.full((LANES,), slot, jnp.float32)
    send[:, pl.ds((blocks + 2) * nodes, META), :] = meta[...].astype(jnp.bfloat16)


def dot(a, b, contract, precision=None):
    return lax.dot_general(
        a, b, (contract, ((), ())), precision=precision, preferred_element_type=jnp.float32
    )


def step_kernel(
    core, weights, recv, kept, given,
    slots, slot_ids, h0, p0, p1, h1, adj, active, acc, pooled, slot_sem,
):
    count = recv.shape[0]
    columns = weights.shape[1]
    blocks = columns // LANES
    nodes = adj.shape[1]
    body = (blocks + 2) * nodes
    rows = 2 * nodes
    low = jnp.bfloat16

    slots[...] = recv[:, pl.ds(body, META), :].astype(jnp.float32)
    pooled[2, :, pl.ds(0, LANES)] = slots[:, 2 * blocks + 2, :]
    nbr = slots[:, 2 * blocks + 2, :].astype(jnp.int32) - 1
    own = lax.broadcasted_iota(jnp.int32, nbr.shape, 0)
    linked = jnp.where(nbr < 0, own, nbr)

    def put_ids(ids_vmem):
        ids_vmem[...] = linked
        copy = pltpu.make_async_copy(ids_vmem, slot_ids, slot_sem)
        copy.start()
        copy.wait()

    pl.run_scoped(put_ids, pltpu.VMEM((count, LANES), jnp.int32))

    def project(s, carry):
        n = slot_ids[s, 0]
        own_rows = recv[s, pl.ds(0, blocks * nodes), :].reshape(blocks, nodes, LANES)
        diag = recv[s, pl.ds(blocks * nodes, nodes), :]
        coupling = recv[s, pl.ds((blocks + 1) * nodes, nodes), :]
        zero = jnp.zeros((), low)
        for v in range(2):
            pieces = []
            for j in range(blocks):
                keep = slots[s, pl.ds(v * blocks + j, 1), :] > 0.5
                pieces.append(jnp.where(keep, own_rows[j], zero))
            base = s * rows + v * nodes
            h0[pl.ds(base, nodes), :] = jnp.concatenate(pieces, axis=1)
            own_keep = slots[s, pl.ds(2 * blocks + v, 1), :] > 0.5
            far_keep = slots[n, pl.ds(2 * blocks + v, 1), :] > 0.5
            adj[2 * s + v] = jnp.concatenate(
                [jnp.where(own_keep, diag, zero), jnp.where(far_keep, coupling, zero)], axis=1
            )
        base = s * rows
        p0[pl.ds(base, rows), :] = dot(
            h0[pl.ds(base, rows), :], weights[0], ((1,), (0,))
        ).astype(low)
        acc[pl.ds(base, rows), :] = jnp.zeros((rows, columns), jnp.float32)
        return carry

    lax.fori_loop(0, count, project, 0)

    def gather(source, s, n, v):
        return dot(
            adj[2 * s + v],
            jnp.concatenate(
                [
                    source[pl.ds(s * rows + v * nodes, nodes), :],
                    source[pl.ds(n * rows + v * nodes, nodes), :],
                ],
                axis=0,
            ),
            ((1,), (0,)),
        )

    def first_layer(s, carry):
        n = slot_ids[s, 0]
        for v in range(2):
            h1[pl.ds(s * rows + v * nodes, nodes), :] = jnp.maximum(
                gather(p0, s, n, v), 0.0
            ).astype(low)
        p1[pl.ds(s * rows, rows), :] = dot(
            h1[pl.ds(s * rows, rows), :], weights[1], ((1,), (0,))
        ).astype(low)
        return carry

    lax.fori_loop(0, count, first_layer, 0)

    def second_layer(s, carry):
        n = slot_ids[s, 0]
        for v in range(2):
            summed = jnp.maximum(gather(p1, s, n, v), 0.0)
            active[pl.ds(s * rows + v * nodes, nodes), :] = jnp.where(
                summed > 0, 1.0, 0.0
            ).astype(low)
            pooled[v, pl.ds(s, 1), :] = jnp.sum(summed, axis=0, keepdims=True) * (1.0 / nodes)
        return carry

    lax.fori_loop(0, count, second_layer, 0)

    flags = jnp.where(pooled[2, :, pl.ds(0, LANES)] > 0.5, 1.0, 0.0)
    occ_col = flags[:, 0:1]
    occ_row = dot(
        jnp.full((8, LANES), 1.0 / LANES, jnp.float32), flags, ((1,), (1,)), lax.Precision.HIGHEST
    )[0:1, :]
    means = [pooled[0], pooled[1]]
    inv = [
        lax.rsqrt(jnp.mean(e * e, axis=-1, keepdims=True) + EPSILON) for e in means
    ]
    unit = [e * i for e, i in zip(means, inv)]
    scale = 1.0 / (columns * SOFTMAX_TEMPER)
    high = lax.Precision.HIGHEST
    scores = dot(unit[0], unit[1], ((1,), (1,)), high) * scale
    weighted = jnp.exp(scores) * occ_row
    totals = jnp.where(occ_col > 0.5, jnp.sum(weighted, axis=1, keepdims=True), 1.0)
    row_id = lax.broadcasted_iota(jnp.int32, (count, count), 0)
    col_id = lax.broadcasted_iota(jnp.int32, (count, count), 1)
    eye = jnp.where(row_id == col_id, 1.0, 0.0)
    coeffs = (weighted / totals - eye) * occ_col
    unit_grad = [
        dot(coeffs, unit[1], ((1,), (0,)), high) * scale,
        dot(coeffs, unit[0], ((0,), (0,)), high) * scale,
    ]
    for v in range(2):
        grad = (
            inv[v] * unit_grad[v]
            - (inv[v] ** 3 * jnp.sum(means[v] * unit_grad[v], axis=-1, keepdims=True) / columns)
            * means[v]
        )
        pooled[v] = (grad / nodes).astype(low).astype(jnp.float32)

    def scatter(s, v, grad):
        n = slot_ids[s, 0]
        spread = dot(adj[2 * s + v], grad, ((0,), (0,)))
        mine = pl.ds(s * rows + v * nodes, nodes)
        acc[mine, :] = acc[mine, :] + spread[:nodes]
        far = pl.ds(n * rows + v * nodes, nodes)
        acc[far, :] = acc[far, :] + spread[nodes:]

    def second_back(s, carry):
        for v in range(2):
            row = pooled[v, pl.ds(s, 1), :].astype(low)
            scatter(s, v, active[pl.ds(s * rows + v * nodes, nodes), :] * row)
        return carry

    lax.fori_loop(0, count, second_back, 0)

    chunk = 4 * rows
    kept[...] = jnp.zeros_like(kept)
    given[...] = jnp.zeros_like(given)

    def add(layer, part):
        @pl.when(core[0] == layer)
        def _():
            kept[...] = kept[...] + part

        @pl.when(core[0] != layer)
        def _():
            given[...] = given[...] + part

    def second_weights(i, carry):
        span = pl.ds(i * chunk, chunk)
        grad = acc[span, :].astype(low)
        acc[span, :] = jnp.zeros((chunk, columns), jnp.float32)
        hidden = h1[span, :]
        add(1, dot(hidden, grad, ((0,), (0,))))
        below = dot(grad, weights[1], ((1,), (1,)))
        p0[span, :] = jnp.where(hidden > 0, below, 0.0).astype(low)
        return carry

    lax.fori_loop(0, count // 4, second_weights, 0)

    def first_back(s, carry):
        for v in range(2):
            scatter(s, v, p0[pl.ds(s * rows + v * nodes, nodes), :])
        return carry

    lax.fori_loop(0, count, first_back, 0)

    def first_weights(i, carry):
        span = pl.ds(i * chunk, chunk)
        add(0, dot(h0[span, :], acc[span, :].astype(low), ((0,), (0,))))
        return carry

    lax.fori_loop(0, count // 4, first_weights, 0)


def local(
    features, diag_blocks, coupling_blocks, neighbour, assignment, feature_drop, edge_drop, weights
):
    count = lax.axis_size("batch")
    stores = lax.axis_size("store")
    _, owned, nodes, columns = features.shape
    blocks = columns // LANES
    body = (blocks + 2) * nodes
    low = jnp.bfloat16
    smem = pl.BlockSpec(memory_space=pltpu.SMEM)
    vmem = pl.BlockSpec(memory_space=pltpu.VMEM)
    send = pl.pallas_call(
        pack_kernel,
        out_shape=jax.ShapeDtypeStruct((count, body + META, LANES), low),
        in_specs=[smem, smem, vmem, vmem, vmem, vmem, vmem],
        out_specs=vmem,
        scratch_shapes=[pltpu.VMEM((count, META, LANES), jnp.float32)],
        name="pack",
    )(assignment, neighbour, features, diag_blocks, coupling_blocks, feature_drop, edge_drop)
    parity = lax.axis_index("store") % 2
    send, parity = lax.optimization_barrier((send, parity))
    recv = lax.all_to_all(send, "batch", split_axis=0, concat_axis=0, tiled=True)
    total = count * 2 * nodes
    half = jax.ShapeDtypeStruct((columns, columns), jnp.float32)
    kept, given = pl.pallas_call(
        step_kernel,
        out_shape=[half, half],
        in_specs=[smem, vmem, vmem],
        out_specs=[vmem, vmem],
        scratch_shapes=[
            pltpu.VMEM((count, META, LANES), jnp.float32),
            pltpu.SMEM((count, LANES), jnp.int32),
            pltpu.VMEM((total, columns), low),
            pltpu.VMEM((total, columns), low),
            pltpu.VMEM((total, columns), low),
            pltpu.VMEM((total, columns), low),
            pltpu.VMEM((2 * count, nodes, 2 * nodes), low),
            pltpu.VMEM((total, columns), low),
            pltpu.VMEM((total, columns), jnp.float32),
            pltpu.VMEM((3, count, columns), jnp.float32),
            pltpu.SemaphoreType.DMA,
        ],
        compiler_params=pltpu.CompilerParams(vmem_limit_bytes=56 << 20),
        name="step",
    )(parity.reshape(1).astype(jnp.int32), weights, recv)

    swap = [(s, s ^ 1) for s in range(stores)]
    kept = kept + lax.ppermute(given, "store", swap)
    chips = stores // 2 * count
    groups = [
        [s * count + b for s in range(c, stores, 2) for b in range(count)] for c in range(2)
    ]
    axes = ("store", "batch")
    pieces = lax.all_to_all(
        kept.reshape(chips, columns // chips, columns),
        axes, split_axis=0, concat_axis=0, axis_index_groups=groups, tiled=True,
    )
    piece = jnp.sum(pieces, axis=0).astype(low)
    layer = lax.all_to_all(
        jnp.broadcast_to(piece[None], (chips,) + piece.shape),
        axes, split_axis=0, concat_axis=0, axis_index_groups=groups, tiled=True,
    ).reshape(columns, columns)
    other = lax.ppermute(layer, "store", swap)
    first = parity == 0
    return jnp.stack(
        [jnp.where(first, layer, other), jnp.where(first, other, layer)]
    ).astype(jnp.float32)


def solution(mesh):
    return jax.shard_map(
        local,
        mesh=mesh,
        in_specs=(
            P("store", "batch", None, None),
            P("store", "batch", None, None),
            P("store", "batch", None, None),
            P("store", "batch"),
            P("store", "batch"),
            P("store", "batch", None, None),
            P("store", "batch", None, None),
            P(),
        ),
        out_specs=P(),
        check_vma=False,
    )
```

```python
import jax
import jax.numpy as jnp
from jax import lax
from jax.experimental import pallas as pl
from jax.experimental.pallas import tpu as pltpu
from jax.sharding import PartitionSpec as P

SOFTMAX_TEMPER = 0.5
EPSILON = 1e-05

LANES = 128
META = 16
UA = 8
UB = 16
UC = 16
CHUNK = 16


def pack_kernel(
    assign, neighbour, features, diag, coupling, feature_drop, edge_drop, send, meta
):
    owned, nodes, columns = features.shape[1:]
    blocks = columns // LANES
    meta[...] = jnp.zeros_like(meta)
    send[:, pl.ds(0, (blocks + 2) * nodes), :] = jnp.zeros(
        (send.shape[0], (blocks + 2) * nodes, LANES), jnp.bfloat16
    )
    for k in range(owned):
        target = assign[0, k]
        for j in range(blocks):
            send[target, pl.ds(j * nodes, nodes), :] = features[0, k, :, pl.ds(j * LANES, LANES)]
        send[target, pl.ds(blocks * nodes, nodes), :] = diag[0, k]
        send[target, pl.ds((blocks + 1) * nodes, nodes), :] = coupling[0, k]
        for v in range(2):
            for j in range(blocks):
                meta[target, v * blocks + j, :] = feature_drop[
                    0, k, v, pl.ds(j * LANES, LANES)
                ].astype(jnp.float32)
            meta[target, 2 * blocks + v, :] = edge_drop[0, k, v, :].astype(jnp.float32)
        slot = neighbour[0, k] // owned + 1
        meta[target, 2 * blocks + 2, :] = jnp.full((LANES,), slot, jnp.float32)
    send[:, pl.ds((blocks + 2) * nodes, META), :] = meta[...].astype(jnp.bfloat16)


def dot(a, b, contract, precision=None):
    return lax.dot_general(
        a, b, (contract, ((), ())), precision=precision, preferred_element_type=jnp.float32
    )


def step_kernel(
    core, weights, recv, kept, given,
    slots, links, first, extra_count, extra_to, extra_from,
    h0, p0, p1, h1, near, far, active, sums, pooled, link_sem,
):
    count = recv.shape[0]
    columns = weights.shape[1]
    blocks = columns // LANES
    nodes = near.shape[1]
    body = (blocks + 2) * nodes
    rows = 2 * nodes
    chunk = sums.shape[0] // rows
    low = jnp.bfloat16

    slots[...] = recv[:, pl.ds(body, META), :].astype(jnp.float32)
    pooled[2, :, pl.ds(0, LANES)] = slots[:, 2 * blocks + 2, :]
    found = slots[:, 2 * blocks + 2, :].astype(jnp.int32) - 1
    itself = lax.broadcasted_iota(jnp.int32, found.shape, 0)

    def put_links(staged):
        staged[...] = jnp.where(found < 0, itself, found)
        copy = pltpu.make_async_copy(staged, links, link_sem)
        copy.start()
        copy.wait()

    pl.run_scoped(put_links, pltpu.VMEM((count, LANES), jnp.int32))

    for s in range(count):
        first[s] = count
    for i in range(count // chunk):
        extra_count[i] = 0

    def enlist(s, carry):
        n = links[s, 0]
        i = n // chunk
        taken = first[n] != count

        @pl.when(taken)
        def _():
            k = extra_count[i]
            extra_to[i * count + k] = n
            extra_from[i * count + k] = s
            extra_count[i] = k + 1

        @pl.when(jnp.logical_not(taken))
        def _():
            first[n] = s

        return carry

    lax.fori_loop(0, count, enlist, 0)
    far[pl.ds(2 * count, 2)] = jnp.zeros((2, nodes, nodes), low)

    def each(width, stage, then=None):
        def steps(i, carry):
            for u in range(width):
                stage(i * width + u)
            if then is not None:
                then(pl.ds(i * width * rows, width * rows))
            return carry

        lax.fori_loop(0, count // width, steps, 0)

    def part(s, v):
        return pl.ds(s * rows + v * nodes, nodes)

    def project(s):
        n = links[s, 0]
        for v in range(2):
            pieces = []
            for j in range(blocks):
                keep = slots[s, pl.ds(v * blocks + j, 1), :].astype(low)
                pieces.append(recv[s, pl.ds(j * nodes, nodes), :] * keep)
            h0[part(s, v), :] = jnp.concatenate(pieces, axis=1)
            own_keep = slots[s, pl.ds(2 * blocks + v, 1), :].astype(low)
            far_keep = slots[n, pl.ds(2 * blocks + v, 1), :].astype(low)
            near[2 * s + v] = recv[s, pl.ds(blocks * nodes, nodes), :] * own_keep
            far[2 * s + v] = recv[s, pl.ds((blocks + 1) * nodes, nodes), :] * far_keep

    def project_rows(span):
        p0[span, :] = dot(h0[span, :], weights[0], ((1,), (0,))).astype(low)

    each(UA, project, project_rows)

    def gather(source, s, v):
        n = links[s, 0]
        return dot(
            jnp.concatenate([near[2 * s + v], far[2 * s + v]], axis=1),
            jnp.concatenate([source[part(s, v), :], source[part(n, v), :]], axis=0),
            ((1,), (0,)),
        )

    def first_layer(s):
        for v in range(2):
            h1[part(s, v), :] = jnp.maximum(gather(p0, s, v), 0.0).astype(low)

    def first_rows(span):
        p1[span, :] = dot(h1[span, :], weights[1], ((1,), (0,))).astype(low)

    each(UB, first_layer, first_rows)

    def second_layer(s):
        for v in range(2):
            summed = jnp.maximum(gather(p1, s, v), 0.0)
            active[part(s, v), :] = jnp.where(summed > 0, 1.0, 0.0).astype(low)
            pooled[v, pl.ds(s, 1), :] = jnp.sum(summed, axis=0, keepdims=True) * (1.0 / nodes)

    each(UC, second_layer)

    flags = jnp.where(pooled[2, :, pl.ds(0, LANES)] > 0.5, 1.0, 0.0)
    occ_col = flags[:, 0:1]
    occ_row = dot(
        jnp.full((8, LANES), 1.0 / LANES, jnp.float32), flags, ((1,), (1,)), lax.Precision.HIGHEST
    )[0:1, :]
    means = [pooled[0], pooled[1]]
    inv = [lax.rsqrt(jnp.mean(e * e, axis=-1, keepdims=True) + EPSILON) for e in means]
    unit = [e * i for e, i in zip(means, inv)]
    scale = 1.0 / (columns * SOFTMAX_TEMPER)
    high = lax.Precision.HIGHEST
    scores = dot(unit[0], unit[1], ((1,), (1,)), high) * scale
    weighted = jnp.exp(scores) * occ_row
    totals = jnp.where(occ_col > 0.5, jnp.sum(weighted, axis=1, keepdims=True), 1.0)
    row_id = lax.broadcasted_iota(jnp.int32, (count, count), 0)
    col_id = lax.broadcasted_iota(jnp.int32, (count, count), 1)
    eye = jnp.where(row_id == col_id, 1.0, 0.0)
    coeffs = (weighted / totals - eye) * occ_col
    unit_grad = [
        dot(coeffs, unit[1], ((1,), (0,)), high) * scale,
        dot(coeffs, unit[0], ((0,), (0,)), high) * scale,
    ]
    for v in range(2):
        grad = (
            inv[v] * unit_grad[v]
            - (inv[v] ** 3 * jnp.sum(means[v] * unit_grad[v], axis=-1, keepdims=True) / columns)
            * means[v]
        )
        pooled[v] = (grad / nodes).astype(low).astype(jnp.float32)

    def add(layer, part_sum):
        @pl.when(core[0] == layer)
        def _():
            kept[...] = kept[...] + part_sum

        @pl.when(core[0] != layer)
        def _():
            given[...] = given[...] + part_sum

    kept[...] = jnp.zeros_like(kept)
    given[...] = jnp.zeros_like(given)

    def spread(i, grad_of):
        for u in range(chunk):
            s = i * chunk + u
            a = first[s]
            b = jnp.minimum(a, count - 1)
            for v in range(2):
                sums[pl.ds(u * rows + v * nodes, nodes), :] = dot(
                    jnp.concatenate([near[2 * s + v], far[2 * a + v]], axis=0),
                    jnp.concatenate([grad_of(s, v), grad_of(b, v)], axis=0),
                    ((0,), (0,)),
                )

        def further(k, carry):
            a = extra_from[i * count + k]
            u = extra_to[i * count + k] - i * chunk
            for v in range(2):
                mine = part(u, v)
                sums[mine, :] = sums[mine, :] + dot(far[2 * a + v], grad_of(a, v), ((0,), (0,)))
            return carry

        lax.fori_loop(0, extra_count[i], further, 0)
        return sums[...].astype(low)

    def second_grad(s, v):
        return active[part(s, v), :] * pooled[v, pl.ds(s, 1), :].astype(low)

    def second_back(i, carry):
        grad = spread(i, second_grad)
        span = pl.ds(i * chunk * rows, chunk * rows)
        hidden = h1[span, :]
        add(1, dot(hidden, grad, ((0,), (0,))))
        below = dot(grad, weights[1], ((1,), (1,)))
        p0[span, :] = jnp.where(hidden > 0, below, 0.0).astype(low)
        return carry

    lax.fori_loop(0, count // chunk, second_back, 0)

    def first_grad(s, v):
        return p0[part(s, v), :]

    def first_back(i, carry):
        grad = spread(i, first_grad)
        add(0, dot(h0[pl.ds(i * chunk * rows, chunk * rows), :], grad, ((0,), (0,))))
        return carry

    lax.fori_loop(0, count // chunk, first_back, 0)


def local(
    features, diag_blocks, coupling_blocks, neighbour, assignment, feature_drop, edge_drop, weights
):
    count = lax.axis_size("batch")
    stores = lax.axis_size("store")
    _, owned, nodes, columns = features.shape
    blocks = columns // LANES
    body = (blocks + 2) * nodes
    low = jnp.bfloat16
    smem = pl.BlockSpec(memory_space=pltpu.SMEM)
    vmem = pl.BlockSpec(memory_space=pltpu.VMEM)
    send = pl.pallas_call(
        pack_kernel,
        out_shape=jax.ShapeDtypeStruct((count, body + META, LANES), low),
        in_specs=[smem, smem, vmem, vmem, vmem, vmem, vmem],
        out_specs=vmem,
        scratch_shapes=[pltpu.VMEM((count, META, LANES), jnp.float32)],
        name="pack",
    )(assignment, neighbour, features, diag_blocks, coupling_blocks, feature_drop, edge_drop)
    parity = lax.axis_index("store") % 2
    send, parity = lax.optimization_barrier((send, parity))
    recv = lax.all_to_all(send, "batch", split_axis=0, concat_axis=0, tiled=True)
    total = count * 2 * nodes
    half = jax.ShapeDtypeStruct((columns, columns), jnp.float32)
    kept, given = pl.pallas_call(
        step_kernel,
        out_shape=[half, half],
        in_specs=[smem, vmem, vmem],
        out_specs=[vmem, vmem],
        scratch_shapes=[
            pltpu.VMEM((count, META, LANES), jnp.float32),
            pltpu.SMEM((count, LANES), jnp.int32),
            pltpu.SMEM((count,), jnp.int32),
            pltpu.SMEM((count,), jnp.int32),
            pltpu.SMEM((count * count,), jnp.int32),
            pltpu.SMEM((count * count,), jnp.int32),
            pltpu.VMEM((total, columns), low),
            pltpu.VMEM((total, columns), low),
            pltpu.VMEM((total, columns), low),
            pltpu.VMEM((total, columns), low),
            pltpu.VMEM((2 * count, nodes, nodes), low),
            pltpu.VMEM((2 * count + 2, nodes, nodes), low),
            pltpu.VMEM((total, columns), low),
            pltpu.VMEM((CHUNK * 2 * nodes, columns), jnp.float32),
            pltpu.VMEM((3, count, columns), jnp.float32),
            pltpu.SemaphoreType.DMA,
        ],
        compiler_params=pltpu.CompilerParams(vmem_limit_bytes=56 << 20),
        name="step",
    )(parity.reshape(1).astype(jnp.int32), weights, recv)

    swap = [(s, s ^ 1) for s in range(stores)]
    kept = kept + lax.ppermute(given, "store", swap)
    chips = stores // 2 * count
    groups = [
        [s * count + b for s in range(c, stores, 2) for b in range(count)] for c in range(2)
    ]
    axes = ("store", "batch")
    pieces = lax.all_to_all(
        kept.reshape(chips, columns // chips, columns),
        axes, split_axis=0, concat_axis=0, axis_index_groups=groups, tiled=True,
    )
    piece = jnp.sum(pieces, axis=0).astype(low)
    layer = lax.all_to_all(
        jnp.broadcast_to(piece[None], (chips,) + piece.shape),
        axes, split_axis=0, concat_axis=0, axis_index_groups=groups, tiled=True,
    ).reshape(columns, columns)
    other = lax.ppermute(layer, "store", swap)
    first = parity == 0
    return jnp.stack(
        [jnp.where(first, layer, other), jnp.where(first, other, layer)]
    ).astype(jnp.float32)


def solution(mesh):
    return jax.shard_map(
        local,
        mesh=mesh,
        in_specs=(
            P("store", "batch", None, None),
            P("store", "batch", None, None),
            P("store", "batch", None, None),
            P("store", "batch"),
            P("store", "batch"),
            P("store", "batch", None, None),
            P("store", "batch", None, None),
            P(),
        ),
        out_specs=P(),
        check_vma=False,
    )
```

```python
import jax
import jax.numpy as jnp
from jax import lax
from jax.experimental import pallas as pl
from jax.experimental.pallas import tpu as pltpu
from jax.sharding import PartitionSpec as P

SOFTMAX_TEMPER = 0.5
EPSILON = 1e-05

LANES = 128
META = 16
UA = 8
UB = 16
UC = 16
CHUNK = 16


def pack_kernel(
    assign, neighbour, features, diag, coupling, feature_drop, edge_drop, send, meta
):
    owned, nodes, columns = features.shape[1:]
    blocks = columns // LANES
    meta[...] = jnp.zeros_like(meta)
    send[:, pl.ds(0, (blocks + 2) * nodes), :] = jnp.zeros(
        (send.shape[0], (blocks + 2) * nodes, LANES), jnp.bfloat16
    )
    for k in range(owned):
        target = assign[0, k]
        for j in range(blocks):
            send[target, pl.ds(j * nodes, nodes), :] = features[0, k, :, pl.ds(j * LANES, LANES)]
        send[target, pl.ds(blocks * nodes, nodes), :] = diag[0, k]
        send[target, pl.ds((blocks + 1) * nodes, nodes), :] = coupling[0, k]
        for v in range(2):
            for j in range(blocks):
                meta[target, v * blocks + j, :] = feature_drop[
                    0, k, v, pl.ds(j * LANES, LANES)
                ].astype(jnp.float32)
            meta[target, 2 * blocks + v, :] = edge_drop[0, k, v, :].astype(jnp.float32)
        slot = neighbour[0, k] // owned + 1
        meta[target, 2 * blocks + 2, :] = jnp.full((LANES,), slot, jnp.float32)
    send[:, pl.ds((blocks + 2) * nodes, META), :] = meta[...].astype(jnp.bfloat16)


def dot(a, b, contract, precision=None):
    return lax.dot_general(
        a, b, (contract, ((), ())), precision=precision, preferred_element_type=jnp.float32
    )


def step_kernel(
    core, weights, recv, kept, given,
    slots, links, first, extra_count, extra_to, extra_from,
    h0, p0, p1, h1, near, far, active, sums, pooled, link_sem,
):
    count = recv.shape[0]
    columns = weights.shape[1]
    blocks = columns // LANES
    nodes = near.shape[1]
    body = (blocks + 2) * nodes
    rows = 2 * nodes
    chunk = sums.shape[0] // rows
    low = jnp.bfloat16

    slots[...] = recv[:, pl.ds(body, META), :].astype(jnp.float32)
    pooled[2, :, pl.ds(0, LANES)] = slots[:, 2 * blocks + 2, :]
    found = slots[:, 2 * blocks + 2, :].astype(jnp.int32) - 1
    itself = lax.broadcasted_iota(jnp.int32, found.shape, 0)

    def put_links(staged):
        staged[...] = jnp.where(found < 0, itself, found)
        copy = pltpu.make_async_copy(staged, links, link_sem)
        copy.start()
        copy.wait()

    pl.run_scoped(put_links, pltpu.VMEM((count, LANES), jnp.int32))

    for s in range(count):
        first[s] = count
    for i in range(count // chunk):
        extra_count[i] = 0

    def enlist(s, carry):
        n = links[s, 0]
        i = n // chunk
        taken = first[n] != count

        @pl.when(taken)
        def _():
            k = extra_count[i]
            extra_to[i * count + k] = n
            extra_from[i * count + k] = s
            extra_count[i] = k + 1

        @pl.when(jnp.logical_not(taken))
        def _():
            first[n] = s

        return carry

    lax.fori_loop(0, count, enlist, 0)
    far[pl.ds(2 * count, 2)] = jnp.zeros((2, nodes, nodes), low)

    def each(width, stage, then=None):
        def steps(i, carry):
            for u in range(width):
                stage(i * width + u)
            if then is not None:
                then(pl.ds(i * width * rows, width * rows))
            return carry

        lax.fori_loop(0, count // width, steps, 0)

    def part(s, v):
        return pl.ds(s * rows + v * nodes, nodes)

    def project(s):
        n = links[s, 0]
        for v in range(2):
            pieces = []
            for j in range(blocks):
                keep = slots[s, pl.ds(v * blocks + j, 1), :].astype(low)
                pieces.append(recv[s, pl.ds(j * nodes, nodes), :] * keep)
            h0[part(s, v), :] = jnp.concatenate(pieces, axis=1)
            own_keep = slots[s, pl.ds(2 * blocks + v, 1), :].astype(low)
            far_keep = slots[n, pl.ds(2 * blocks + v, 1), :].astype(low)
            near[2 * s + v] = recv[s, pl.ds(blocks * nodes, nodes), :] * own_keep
            far[2 * s + v] = recv[s, pl.ds((blocks + 1) * nodes, nodes), :] * far_keep

    def project_rows(span):
        p0[span, :] = dot(h0[span, :], weights[0], ((1,), (0,))).astype(low)

    each(UA, project, project_rows)

    def gather(source, s, v):
        n = links[s, 0]
        return dot(
            jnp.concatenate([near[2 * s + v], far[2 * s + v]], axis=1),
            jnp.concatenate([source[part(s, v), :], source[part(n, v), :]], axis=0),
            ((1,), (0,)),
        )

    def first_layer(s):
        for v in range(2):
            h1[part(s, v), :] = jnp.maximum(gather(p0, s, v), 0.0).astype(low)

    def first_rows(span):
        p1[span, :] = dot(h1[span, :], weights[1], ((1,), (0,))).astype(low)

    each(UB, first_layer, first_rows)

    def second_layer(s):
        for v in range(2):
            summed = jnp.maximum(gather(p1, s, v), 0.0)
            active[part(s, v), :] = jnp.where(summed > 0, 1.0, 0.0).astype(low)
            pooled[v, pl.ds(s, 1), :] = jnp.sum(summed, axis=0, keepdims=True) * (1.0 / nodes)

    each(UC, second_layer)

    flags = jnp.where(pooled[2, :, pl.ds(0, LANES)] > 0.5, 1.0, 0.0)
    occ_col = flags[:, 0:1]
    occ_row = dot(
        jnp.full((8, LANES), 1.0 / LANES, jnp.float32), flags, ((1,), (1,)), lax.Precision.HIGHEST
    )[0:1, :]
    means = [pooled[0], pooled[1]]
    inv = [lax.rsqrt(jnp.mean(e * e, axis=-1, keepdims=True) + EPSILON) for e in means]
    unit = [e * i for e, i in zip(means, inv)]
    scale = 1.0 / (columns * SOFTMAX_TEMPER)
    high = lax.Precision.HIGHEST
    scores = dot(unit[0], unit[1], ((1,), (1,)), high) * scale
    weighted = jnp.exp(scores) * occ_row
    totals = jnp.where(occ_col > 0.5, jnp.sum(weighted, axis=1, keepdims=True), 1.0)
    row_id = lax.broadcasted_iota(jnp.int32, (count, count), 0)
    col_id = lax.broadcasted_iota(jnp.int32, (count, count), 1)
    eye = jnp.where(row_id == col_id, 1.0, 0.0)
    coeffs = (weighted / totals - eye) * occ_col
    unit_grad = [
        dot(coeffs, unit[1], ((1,), (0,)), high) * scale,
        dot(coeffs, unit[0], ((0,), (0,)), high) * scale,
    ]
    for v in range(2):
        grad = (
            inv[v] * unit_grad[v]
            - (inv[v] ** 3 * jnp.sum(means[v] * unit_grad[v], axis=-1, keepdims=True) / columns)
            * means[v]
        )
        pooled[v] = (grad / nodes).astype(low).astype(jnp.float32)

    def add(layer, part_sum):
        @pl.when(core[0] == layer)
        def _():
            kept[...] = kept[...] + part_sum

        @pl.when(core[0] != layer)
        def _():
            given[...] = given[...] + part_sum

    kept[...] = jnp.zeros_like(kept)
    given[...] = jnp.zeros_like(given)

    def spread(i, grad_of):
        for u in range(chunk):
            s = i * chunk + u
            a = first[s]
            b = jnp.minimum(a, count - 1)
            for v in range(2):
                sums[pl.ds(u * rows + v * nodes, nodes), :] = dot(
                    jnp.concatenate([near[2 * s + v], far[2 * a + v]], axis=0),
                    jnp.concatenate([grad_of(s, v), grad_of(b, v)], axis=0),
                    ((0,), (0,)),
                )

        def further(k, carry):
            a = extra_from[i * count + k]
            u = extra_to[i * count + k] - i * chunk
            for v in range(2):
                mine = part(u, v)
                sums[mine, :] = sums[mine, :] + dot(far[2 * a + v], grad_of(a, v), ((0,), (0,)))
            return carry

        lax.fori_loop(0, extra_count[i], further, 0)
        return sums[...].astype(low)

    def second_grad(s, v):
        return active[part(s, v), :] * pooled[v, pl.ds(s, 1), :].astype(low)

    def second_back(i, carry):
        grad = spread(i, second_grad)
        span = pl.ds(i * chunk * rows, chunk * rows)
        hidden = h1[span, :]
        add(1, dot(hidden, grad, ((0,), (0,))))
        below = dot(grad, weights[1], ((1,), (1,)))
        p0[span, :] = jnp.where(hidden > 0, below, 0.0).astype(low)
        return carry

    lax.fori_loop(0, count // chunk, second_back, 0)

    def first_grad(s, v):
        return p0[part(s, v), :]

    def first_back(i, carry):
        grad = spread(i, first_grad)
        add(0, dot(h0[pl.ds(i * chunk * rows, chunk * rows), :], grad, ((0,), (0,))))
        return carry

    lax.fori_loop(0, count // chunk, first_back, 0)


def local(
    features, diag_blocks, coupling_blocks, neighbour, assignment, feature_drop, edge_drop, weights
):
    count = lax.axis_size("batch")
    stores = lax.axis_size("store")
    _, owned, nodes, columns = features.shape
    blocks = columns // LANES
    body = (blocks + 2) * nodes
    low = jnp.bfloat16
    smem = pl.BlockSpec(memory_space=pltpu.SMEM)
    vmem = pl.BlockSpec(memory_space=pltpu.VMEM)
    send = pl.pallas_call(
        pack_kernel,
        out_shape=jax.ShapeDtypeStruct((count, body + META, LANES), low),
        in_specs=[smem, smem, vmem, vmem, vmem, vmem, vmem],
        out_specs=vmem,
        scratch_shapes=[pltpu.VMEM((count, META, LANES), jnp.float32)],
        compiler_params=pltpu.CompilerParams(vmem_limit_bytes=16 << 20),
        name="pack",
    )(assignment, neighbour, features, diag_blocks, coupling_blocks, feature_drop, edge_drop)
    parity = lax.axis_index("store") % 2
    send, parity = lax.optimization_barrier((send, parity))
    recv = lax.all_to_all(send, "batch", split_axis=0, concat_axis=0, tiled=True)
    total = count * 2 * nodes
    half = jax.ShapeDtypeStruct((columns, columns), jnp.float32)
    kept, given = pl.pallas_call(
        step_kernel,
        out_shape=[half, half],
        in_specs=[smem, vmem, vmem],
        out_specs=[vmem, vmem],
        scratch_shapes=[
            pltpu.VMEM((count, META, LANES), jnp.float32),
            pltpu.SMEM((count, LANES), jnp.int32),
            pltpu.SMEM((count,), jnp.int32),
            pltpu.SMEM((count,), jnp.int32),
            pltpu.SMEM((count * count,), jnp.int32),
            pltpu.SMEM((count * count,), jnp.int32),
            pltpu.VMEM((total, columns), low),
            pltpu.VMEM((total, columns), low),
            pltpu.VMEM((total, columns), low),
            pltpu.VMEM((total, columns), low),
            pltpu.VMEM((2 * count, nodes, nodes), low),
            pltpu.VMEM((2 * count + 2, nodes, nodes), low),
            pltpu.VMEM((total, columns), low),
            pltpu.VMEM((CHUNK * 2 * nodes, columns), jnp.float32),
            pltpu.VMEM((3, count, columns), jnp.float32),
            pltpu.SemaphoreType.DMA,
        ],
        compiler_params=pltpu.CompilerParams(vmem_limit_bytes=46 << 20),
        name="step",
    )(parity.reshape(1).astype(jnp.int32), weights, recv)

    swap = [(s, s ^ 1) for s in range(stores)]
    kept = kept + lax.ppermute(given, "store", swap)
    chips = stores // 2 * count
    groups = [
        [s * count + b for s in range(c, stores, 2) for b in range(count)] for c in range(2)
    ]
    axes = ("store", "batch")
    pieces = lax.all_to_all(
        kept.reshape(chips, columns // chips, columns),
        axes, split_axis=0, concat_axis=0, axis_index_groups=groups, tiled=True,
    )
    piece = jnp.sum(pieces, axis=0).astype(low)
    layer = lax.all_to_all(
        jnp.broadcast_to(piece[None], (chips,) + piece.shape),
        axes, split_axis=0, concat_axis=0, axis_index_groups=groups, tiled=True,
    ).reshape(columns, columns)
    other = lax.ppermute(layer, "store", swap)
    first = parity == 0
    return jnp.stack(
        [jnp.where(first, layer, other), jnp.where(first, other, layer)]
    ).astype(jnp.float32)


def solution(mesh):
    return jax.shard_map(
        local,
        mesh=mesh,
        in_specs=(
            P("store", "batch", None, None),
            P("store", "batch", None, None),
            P("store", "batch", None, None),
            P("store", "batch"),
            P("store", "batch"),
            P("store", "batch", None, None),
            P("store", "batch", None, None),
            P(),
        ),
        out_specs=P(),
        check_vma=False,
    )
```

```python
import jax
import jax.numpy as jnp
from jax import lax
from jax.experimental import pallas as pl
from jax.experimental.pallas import tpu as pltpu
from jax.sharding import PartitionSpec as P

SOFTMAX_TEMPER = 0.5
EPSILON = 1e-05

LANES = 128
META = 16
UA = 8
UB = 8
UC = 8
UD = 8


def pack_kernel(
    assign, neighbour, features, diag, coupling, feature_drop, edge_drop, send, meta
):
    owned, nodes, columns = features.shape[1:]
    blocks = columns // LANES
    meta[...] = jnp.zeros_like(meta)
    send[:, pl.ds(0, (blocks + 2) * nodes), :] = jnp.zeros(
        (send.shape[0], (blocks + 2) * nodes, LANES), jnp.bfloat16
    )
    for k in range(owned):
        target = assign[0, k]
        for j in range(blocks):
            send[target, pl.ds(j * nodes, nodes), :] = features[0, k, :, pl.ds(j * LANES, LANES)]
        send[target, pl.ds(blocks * nodes, nodes), :] = diag[0, k]
        send[target, pl.ds((blocks + 1) * nodes, nodes), :] = coupling[0, k]
        for v in range(2):
            for j in range(blocks):
                meta[target, v * blocks + j, :] = feature_drop[
                    0, k, v, pl.ds(j * LANES, LANES)
                ].astype(jnp.float32)
            meta[target, 2 * blocks + v, :] = edge_drop[0, k, v, :].astype(jnp.float32)
        slot = neighbour[0, k] // owned + 1
        meta[target, 2 * blocks + 2, :] = jnp.full((LANES,), slot, jnp.float32)
    send[:, pl.ds((blocks + 2) * nodes, META), :] = meta[...].astype(jnp.bfloat16)


def dot(a, b, contract, precision=None):
    return lax.dot_general(
        a, b, (contract, ((), ())), precision=precision, preferred_element_type=jnp.float32
    )


def step_kernel(
    core, weights, recv, out,
    slots, links, first, seen, several, further, shared,
    h0, p0, p1, h1, near, far, active, spread, sums, pooled, link_sem,
):
    count = recv.shape[0]
    columns = weights.shape[1]
    blocks = columns // LANES
    nodes = near.shape[1]
    body = (blocks + 2) * nodes
    rows = 2 * nodes
    low = jnp.bfloat16

    slots[...] = recv[:, pl.ds(body, META), :].astype(jnp.float32)
    pooled[2, :, pl.ds(0, LANES)] = slots[:, 2 * blocks + 2, :]
    found = slots[:, 2 * blocks + 2, :].astype(jnp.int32) - 1
    itself = lax.broadcasted_iota(jnp.int32, found.shape, 0)

    def put_links(staged):
        staged[...] = jnp.where(found < 0, itself, found)
        copy = pltpu.make_async_copy(staged, links, link_sem)
        copy.start()
        copy.wait()

    pl.run_scoped(put_links, pltpu.VMEM((count, LANES), jnp.int32))

    for s in range(count):
        first[s] = count
        seen[s] = 0
    shared[0] = 0

    def enlist(s, carry):
        n = links[s, 0]
        k = seen[n]
        seen[n] = k + 1

        @pl.when(k == 0)
        def _():
            first[n] = s

        @pl.when(k > 0)
        def _():
            further[n * count + k] = s

        @pl.when(k == 1)
        def _():
            several[shared[0]] = n
            shared[0] = shared[0] + 1

        return carry

    lax.fori_loop(0, count, enlist, 0)
    far[pl.ds(2 * count, 2)] = jnp.zeros((2, nodes, nodes), low)

    def each(width, stage, then=None):
        def steps(i, carry):
            for u in range(width):
                stage(i * width + u)
            if then is not None:
                then(pl.ds(i * width * rows, width * rows))
            return carry

        lax.fori_loop(0, count // width, steps, 0)

    def part(s, v):
        return pl.ds(s * rows + v * nodes, nodes)

    def project(s):
        n = links[s, 0]
        for v in range(2):
            pieces = []
            for j in range(blocks):
                keep = slots[s, pl.ds(v * blocks + j, 1), :].astype(low)
                pieces.append(recv[s, pl.ds(j * nodes, nodes), :] * keep)
            h0[part(s, v), :] = jnp.concatenate(pieces, axis=1)
            own_keep = slots[s, pl.ds(2 * blocks + v, 1), :].astype(low)
            far_keep = slots[n, pl.ds(2 * blocks + v, 1), :].astype(low)
            near[2 * s + v] = recv[s, pl.ds(blocks * nodes, nodes), :] * own_keep
            far[2 * s + v] = recv[s, pl.ds((blocks + 1) * nodes, nodes), :] * far_keep

    def project_rows(span):
        p0[span, :] = dot(h0[span, :], weights[0], ((1,), (0,))).astype(low)

    each(UA, project, project_rows)

    def gather(source, s, v):
        n = links[s, 0]
        return dot(
            jnp.concatenate([near[2 * s + v], far[2 * s + v]], axis=1),
            jnp.concatenate([source[part(s, v), :], source[part(n, v), :]], axis=0),
            ((1,), (0,)),
        )

    def first_layer(s):
        for v in range(2):
            h1[part(s, v), :] = jnp.maximum(gather(p0, s, v), 0.0).astype(low)

    def first_rows(span):
        p1[span, :] = dot(h1[span, :], weights[1], ((1,), (0,))).astype(low)

    each(UB, first_layer, first_rows)

    def second_layer(s):
        for v in range(2):
            summed = jnp.maximum(gather(p1, s, v), 0.0)
            active[part(s, v), :] = jnp.where(summed > 0, 1.0, 0.0).astype(low)
            pooled[v, pl.ds(s, 1), :] = jnp.sum(summed, axis=0, keepdims=True) * (1.0 / nodes)

    each(UC, second_layer)

    flags = jnp.where(pooled[2, :, pl.ds(0, LANES)] > 0.5, 1.0, 0.0)
    occ_col = flags[:, 0:1]
    occ_row = dot(
        jnp.full((8, LANES), 1.0 / LANES, jnp.float32), flags, ((1,), (1,)), lax.Precision.HIGHEST
    )[0:1, :]
    means = [pooled[0], pooled[1]]
    inv = [lax.rsqrt(jnp.mean(e * e, axis=-1, keepdims=True) + EPSILON) for e in means]
    unit = [e * i for e, i in zip(means, inv)]
    scale = 1.0 / (columns * SOFTMAX_TEMPER)
    high = lax.Precision.HIGHEST
    scores = dot(unit[0], unit[1], ((1,), (1,)), high) * scale
    weighted = jnp.exp(scores) * occ_row
    totals = jnp.where(occ_col > 0.5, jnp.sum(weighted, axis=1, keepdims=True), 1.0)
    row_id = lax.broadcasted_iota(jnp.int32, (count, count), 0)
    col_id = lax.broadcasted_iota(jnp.int32, (count, count), 1)
    eye = jnp.where(row_id == col_id, 1.0, 0.0)
    coeffs = (weighted / totals - eye) * occ_col
    unit_grad = [
        dot(coeffs, unit[1], ((1,), (0,)), high) * scale,
        dot(coeffs, unit[0], ((0,), (0,)), high) * scale,
    ]
    for v in range(2):
        grad = (
            inv[v] * unit_grad[v]
            - (inv[v] ** 3 * jnp.sum(means[v] * unit_grad[v], axis=-1, keepdims=True) / columns)
            * means[v]
        )
        pooled[v] = (grad / nodes).astype(low).astype(jnp.float32)

    def back(grad_of, hidden, layer):
        def pull(s, v):
            a = first[s]
            b = jnp.minimum(a, count - 1)
            return dot(
                jnp.concatenate([near[2 * s + v], far[2 * a + v]], axis=0),
                jnp.concatenate([grad_of(s, v), grad_of(b, v)], axis=0),
                ((0,), (0,)),
            )

        def straight(s):
            for v in range(2):
                spread[part(s, v), :] = pull(s, v).astype(low)

        each(UD, straight)

        def joined(k, carry):
            c = several[k]
            for v in range(2):
                sums[v] = pull(c, v)

            def more(j, inner):
                a = further[c * count + j]
                for v in range(2):
                    sums[v] = sums[v] + dot(far[2 * a + v], grad_of(a, v), ((0,), (0,)))
                return inner

            lax.fori_loop(1, seen[c], more, 0)
            for v in range(2):
                spread[part(c, v), :] = sums[v].astype(low)
            return carry

        lax.fori_loop(0, shared[0], joined, 0)
        out[core[0] ^ layer] = dot(hidden[...], spread[...], ((0,), (0,)))

    back(
        lambda s, v: active[part(s, v), :] * pooled[v, pl.ds(s, 1), :].astype(low), h1, 1
    )
    below = dot(spread[...], weights[1], ((1,), (1,)))
    p0[...] = jnp.where(h1[...] > 0, below, 0.0).astype(low)
    back(lambda s, v: p0[part(s, v), :], h0, 0)


def local(
    features, diag_blocks, coupling_blocks, neighbour, assignment, feature_drop, edge_drop, weights
):
    count = lax.axis_size("batch")
    stores = lax.axis_size("store")
    _, owned, nodes, columns = features.shape
    blocks = columns // LANES
    body = (blocks + 2) * nodes
    low = jnp.bfloat16
    smem = pl.BlockSpec(memory_space=pltpu.SMEM)
    vmem = pl.BlockSpec(memory_space=pltpu.VMEM)
    send = pl.pallas_call(
        pack_kernel,
        out_shape=jax.ShapeDtypeStruct((count, body + META, LANES), low),
        in_specs=[smem, smem, vmem, vmem, vmem, vmem, vmem],
        out_specs=vmem,
        scratch_shapes=[pltpu.VMEM((count, META, LANES), jnp.float32)],
        name="pack",
    )(assignment, neighbour, features, diag_blocks, coupling_blocks, feature_drop, edge_drop)
    parity = lax.axis_index("store") % 2
    send, parity = lax.optimization_barrier((send, parity))
    recv = lax.all_to_all(send, "batch", split_axis=0, concat_axis=0, tiled=True)
    total = count * 2 * nodes
    halves = pl.pallas_call(
        step_kernel,
        out_shape=jax.ShapeDtypeStruct((2, columns, columns), jnp.float32),
        in_specs=[smem, vmem, vmem],
        out_specs=vmem,
        scratch_shapes=[
            pltpu.VMEM((count, META, LANES), jnp.float32),
            pltpu.SMEM((count, LANES), jnp.int32),
            pltpu.SMEM((count,), jnp.int32),
            pltpu.SMEM((count,), jnp.int32),
            pltpu.SMEM((count,), jnp.int32),
            pltpu.SMEM((count * count,), jnp.int32),
            pltpu.SMEM((1,), jnp.int32),
            pltpu.VMEM((total, columns), low),
            pltpu.VMEM((total, columns), low),
            pltpu.VMEM((total, columns), low),
            pltpu.VMEM((total, columns), low),
            pltpu.VMEM((2 * count, nodes, nodes), low),
            pltpu.VMEM((2 * count + 2, nodes, nodes), low),
            pltpu.VMEM((total, columns), low),
            pltpu.VMEM((total, columns), low),
            pltpu.VMEM((2, nodes, columns), jnp.float32),
            pltpu.VMEM((3, count, columns), jnp.float32),
            pltpu.SemaphoreType.DMA,
        ],
        compiler_params=pltpu.CompilerParams(vmem_limit_bytes=46 << 20),
        name="step",
    )(parity.reshape(1).astype(jnp.int32), weights, recv)

    swap = [(s, s ^ 1) for s in range(stores)]
    kept = halves[0] + lax.ppermute(halves[1], "store", swap)
    chips = stores // 2 * count
    groups = [
        [s * count + b for s in range(c, stores, 2) for b in range(count)] for c in range(2)
    ]
    axes = ("store", "batch")
    pieces = lax.all_to_all(
        kept.reshape(chips, columns // chips, columns),
        axes, split_axis=0, concat_axis=0, axis_index_groups=groups, tiled=True,
    )
    piece = jnp.sum(pieces, axis=0).astype(low)
    layer = lax.all_to_all(
        jnp.broadcast_to(piece[None], (chips,) + piece.shape),
        axes, split_axis=0, concat_axis=0, axis_index_groups=groups, tiled=True,
    ).reshape(columns, columns)
    other = lax.ppermute(layer, "store", swap)
    first = parity == 0
    return jnp.stack(
        [jnp.where(first, layer, other), jnp.where(first, other, layer)]
    ).astype(jnp.float32)


def solution(mesh):
    return jax.shard_map(
        local,
        mesh=mesh,
        in_specs=(
            P("store", "batch", None, None),
            P("store", "batch", None, None),
            P("store", "batch", None, None),
            P("store", "batch"),
            P("store", "batch"),
            P("store", "batch", None, None),
            P("store", "batch", None, None),
            P(),
        ),
        out_specs=P(),
        check_vma=False,
    )
```

```python
import jax
import jax.numpy as jnp
from jax import lax
from jax.experimental import pallas as pl
from jax.experimental.pallas import tpu as pltpu
from jax.sharding import PartitionSpec as P

SOFTMAX_TEMPER = 0.5
EPSILON = 1e-05

LANES = 128
META = 16
UA = 8
UB = 16
UC = 16
CHUNK = 16


def pack_kernel(
    assign, neighbour, features, diag, coupling, feature_drop, edge_drop, send, meta
):
    owned, nodes, columns = features.shape[1:]
    blocks = columns // LANES
    meta[...] = jnp.zeros_like(meta)
    send[:, pl.ds(0, (blocks + 2) * nodes), :] = jnp.zeros(
        (send.shape[0], (blocks + 2) * nodes, LANES), jnp.bfloat16
    )
    for k in range(owned):
        target = assign[0, k]
        for j in range(blocks):
            send[target, pl.ds(j * nodes, nodes), :] = features[0, k, :, pl.ds(j * LANES, LANES)]
        send[target, pl.ds(blocks * nodes, nodes), :] = diag[0, k]
        send[target, pl.ds((blocks + 1) * nodes, nodes), :] = coupling[0, k]
        for v in range(2):
            for j in range(blocks):
                meta[target, v * blocks + j, :] = feature_drop[
                    0, k, v, pl.ds(j * LANES, LANES)
                ].astype(jnp.float32)
            meta[target, 2 * blocks + v, :] = edge_drop[0, k, v, :].astype(jnp.float32)
        slot = neighbour[0, k] // owned + 1
        meta[target, 2 * blocks + 2, :] = jnp.full((LANES,), slot, jnp.float32)
    send[:, pl.ds((blocks + 2) * nodes, META), :] = meta[...].astype(jnp.bfloat16)


def dot(a, b, contract, precision=None):
    return lax.dot_general(
        a, b, (contract, ((), ())), precision=precision, preferred_element_type=jnp.float32
    )


def step_kernel(
    core, weights, recv, out,
    slots, links, first, extra_count, extra_to, extra_from,
    h0, p0, p1, h1, near, far, active, sums, pooled, link_sem,
):
    count = recv.shape[0]
    columns = weights.shape[1]
    blocks = columns // LANES
    nodes = near.shape[1]
    body = (blocks + 2) * nodes
    rows = 2 * nodes
    chunk = sums.shape[0] // rows
    low = jnp.bfloat16

    slots[...] = recv[:, pl.ds(body, META), :].astype(jnp.float32)
    pooled[2, :, pl.ds(0, LANES)] = slots[:, 2 * blocks + 2, :]
    found = slots[:, 2 * blocks + 2, :].astype(jnp.int32) - 1
    itself = lax.broadcasted_iota(jnp.int32, found.shape, 0)

    def put_links(staged):
        staged[...] = jnp.where(found < 0, itself, found)
        copy = pltpu.make_async_copy(staged, links, link_sem)
        copy.start()
        copy.wait()

    pl.run_scoped(put_links, pltpu.VMEM((count, LANES), jnp.int32))

    for s in range(count):
        first[s] = count
    for i in range(count // chunk):
        extra_count[i] = 0

    def enlist(s, carry):
        n = links[s, 0]
        i = n // chunk
        taken = first[n] != count

        @pl.when(taken)
        def _():
            k = extra_count[i]
            extra_to[i * count + k] = n
            extra_from[i * count + k] = s
            extra_count[i] = k + 1

        @pl.when(jnp.logical_not(taken))
        def _():
            first[n] = s

        return carry

    lax.fori_loop(0, count, enlist, 0)
    far[pl.ds(2 * count, 2)] = jnp.zeros((2, nodes, nodes), low)

    def each(width, stage, then=None):
        def steps(i, carry):
            for u in range(width):
                stage(i * width + u)
            if then is not None:
                then(pl.ds(i * width * rows, width * rows))
            return carry

        lax.fori_loop(0, count // width, steps, 0)

    def part(s, v):
        return pl.ds(s * rows + v * nodes, nodes)

    def project(s):
        n = links[s, 0]
        for v in range(2):
            pieces = []
            for j in range(blocks):
                keep = slots[s, pl.ds(v * blocks + j, 1), :].astype(low)
                pieces.append(recv[s, pl.ds(j * nodes, nodes), :] * keep)
            h0[part(s, v), :] = jnp.concatenate(pieces, axis=1)
            own_keep = slots[s, pl.ds(2 * blocks + v, 1), :].astype(low)
            far_keep = slots[n, pl.ds(2 * blocks + v, 1), :].astype(low)
            near[2 * s + v] = recv[s, pl.ds(blocks * nodes, nodes), :] * own_keep
            far[2 * s + v] = recv[s, pl.ds((blocks + 1) * nodes, nodes), :] * far_keep

    def project_rows(span):
        p0[span, :] = dot(h0[span, :], weights[0], ((1,), (0,))).astype(low)

    each(UA, project, project_rows)

    def gather(source, s, v):
        n = links[s, 0]
        return dot(
            jnp.concatenate([near[2 * s + v], far[2 * s + v]], axis=1),
            jnp.concatenate([source[part(s, v), :], source[part(n, v), :]], axis=0),
            ((1,), (0,)),
        )

    def first_layer(s):
        for v in range(2):
            h1[part(s, v), :] = jnp.maximum(gather(p0, s, v), 0.0).astype(low)

    def first_rows(span):
        p1[span, :] = dot(h1[span, :], weights[1], ((1,), (0,))).astype(low)

    each(UB, first_layer, first_rows)

    def second_layer(s):
        for v in range(2):
            summed = jnp.maximum(gather(p1, s, v), 0.0)
            active[part(s, v), :] = jnp.where(summed > 0, 1.0, 0.0).astype(low)
            pooled[v, pl.ds(s, 1), :] = jnp.sum(summed, axis=0, keepdims=True) * (1.0 / nodes)

    each(UC, second_layer)

    flags = jnp.where(pooled[2, :, pl.ds(0, LANES)] > 0.5, 1.0, 0.0)
    occ_col = flags[:, 0:1]
    occ_row = dot(
        jnp.full((8, LANES), 1.0 / LANES, jnp.float32), flags, ((1,), (1,)), lax.Precision.HIGHEST
    )[0:1, :]
    means = [pooled[0], pooled[1]]
    inv = [lax.rsqrt(jnp.mean(e * e, axis=-1, keepdims=True) + EPSILON) for e in means]
    unit = [e * i for e, i in zip(means, inv)]
    scale = 1.0 / (columns * SOFTMAX_TEMPER)
    high = lax.Precision.HIGHEST
    scores = dot(unit[0], unit[1], ((1,), (1,)), high) * scale
    weighted = jnp.exp(scores) * occ_row
    totals = jnp.where(occ_col > 0.5, jnp.sum(weighted, axis=1, keepdims=True), 1.0)
    row_id = lax.broadcasted_iota(jnp.int32, (count, count), 0)
    col_id = lax.broadcasted_iota(jnp.int32, (count, count), 1)
    eye = jnp.where(row_id == col_id, 1.0, 0.0)
    coeffs = (weighted / totals - eye) * occ_col
    unit_grad = [
        dot(coeffs, unit[1], ((1,), (0,)), high) * scale,
        dot(coeffs, unit[0], ((0,), (0,)), high) * scale,
    ]
    for v in range(2):
        grad = (
            inv[v] * unit_grad[v]
            - (inv[v] ** 3 * jnp.sum(means[v] * unit_grad[v], axis=-1, keepdims=True) / columns)
            * means[v]
        )
        pooled[v] = (grad / nodes).astype(low).astype(jnp.float32)

    def spread(i, grad_of):
        for u in range(chunk):
            s = i * chunk + u
            a = first[s]
            b = jnp.minimum(a, count - 1)
            for v in range(2):
                sums[pl.ds(u * rows + v * nodes, nodes), :] = dot(
                    jnp.concatenate([near[2 * s + v], far[2 * a + v]], axis=0),
                    jnp.concatenate([grad_of(s, v), grad_of(b, v)], axis=0),
                    ((0,), (0,)),
                )

        def further(k, carry):
            a = extra_from[i * count + k]
            u = extra_to[i * count + k] - i * chunk
            for v in range(2):
                mine = part(u, v)
                sums[mine, :] = sums[mine, :] + dot(far[2 * a + v], grad_of(a, v), ((0,), (0,)))
            return carry

        lax.fori_loop(0, extra_count[i], further, 0)
        return sums[...].astype(low)

    def second_grad(s, v):
        return active[part(s, v), :] * pooled[v, pl.ds(s, 1), :].astype(low)

    grad = spread(0, second_grad)
    out[core[0] ^ 1] = dot(h1[...], grad, ((0,), (0,)))
    below = dot(grad, weights[1], ((1,), (1,)))
    p0[...] = jnp.where(h1[...] > 0, below, 0.0).astype(low)

    def first_grad(s, v):
        return p0[part(s, v), :]

    out[core[0]] = dot(h0[...], spread(0, first_grad), ((0,), (0,)))


def local(
    features, diag_blocks, coupling_blocks, neighbour, assignment, feature_drop, edge_drop, weights
):
    count = lax.axis_size("batch")
    stores = lax.axis_size("store")
    _, owned, nodes, columns = features.shape
    blocks = columns // LANES
    body = (blocks + 2) * nodes
    low = jnp.bfloat16
    smem = pl.BlockSpec(memory_space=pltpu.SMEM)
    vmem = pl.BlockSpec(memory_space=pltpu.VMEM)
    send = pl.pallas_call(
        pack_kernel,
        out_shape=jax.ShapeDtypeStruct((count, body + META, LANES), low),
        in_specs=[smem, smem, vmem, vmem, vmem, vmem, vmem],
        out_specs=vmem,
        scratch_shapes=[pltpu.VMEM((count, META, LANES), jnp.float32)],
        name="pack",
    )(assignment, neighbour, features, diag_blocks, coupling_blocks, feature_drop, edge_drop)
    parity = lax.axis_index("store") % 2
    send, parity = lax.optimization_barrier((send, parity))
    recv = lax.all_to_all(send, "batch", split_axis=0, concat_axis=0, tiled=True)
    total = count * 2 * nodes
    halves = pl.pallas_call(
        step_kernel,
        out_shape=jax.ShapeDtypeStruct((2, columns, columns), jnp.float32),
        in_specs=[smem, vmem, vmem],
        out_specs=vmem,
        scratch_shapes=[
            pltpu.VMEM((count, META, LANES), jnp.float32),
            pltpu.SMEM((count, LANES), jnp.int32),
            pltpu.SMEM((count,), jnp.int32),
            pltpu.SMEM((count,), jnp.int32),
            pltpu.SMEM((count * count,), jnp.int32),
            pltpu.SMEM((count * count,), jnp.int32),
            pltpu.VMEM((total, columns), low),
            pltpu.VMEM((total, columns), low),
            pltpu.VMEM((total, columns), low),
            pltpu.VMEM((total, columns), low),
            pltpu.VMEM((2 * count, nodes, nodes), low),
            pltpu.VMEM((2 * count + 2, nodes, nodes), low),
            pltpu.VMEM((total, columns), low),
            pltpu.VMEM((CHUNK * 2 * nodes, columns), jnp.float32),
            pltpu.VMEM((3, count, columns), jnp.float32),
            pltpu.SemaphoreType.DMA,
        ],
        compiler_params=pltpu.CompilerParams(vmem_limit_bytes=46 << 20),
        name="step",
    )(parity.reshape(1).astype(jnp.int32), weights, recv)

    swap = [(s, s ^ 1) for s in range(stores)]
    kept = halves[0] + lax.ppermute(halves[1], "store", swap)
    chips = stores // 2 * count
    groups = [
        [s * count + b for s in range(c, stores, 2) for b in range(count)] for c in range(2)
    ]
    axes = ("store", "batch")
    pieces = lax.all_to_all(
        kept.reshape(chips, columns // chips, columns),
        axes, split_axis=0, concat_axis=0, axis_index_groups=groups, tiled=True,
    )
    piece = jnp.sum(pieces, axis=0).astype(low)
    layer = lax.all_to_all(
        jnp.broadcast_to(piece[None], (chips,) + piece.shape),
        axes, split_axis=0, concat_axis=0, axis_index_groups=groups, tiled=True,
    ).reshape(columns, columns)
    other = lax.ppermute(layer, "store", swap)
    first = parity == 0
    return jnp.stack(
        [jnp.where(first, layer, other), jnp.where(first, other, layer)]
    ).astype(jnp.float32)


def solution(mesh):
    return jax.shard_map(
        local,
        mesh=mesh,
        in_specs=(
            P("store", "batch", None, None),
            P("store", "batch", None, None),
            P("store", "batch", None, None),
            P("store", "batch"),
            P("store", "batch"),
            P("store", "batch", None, None),
            P("store", "batch", None, None),
            P(),
        ),
        out_specs=P(),
        check_vma=False,
    )
```

```python
import jax
import jax.numpy as jnp
from jax import lax
from jax.experimental import pallas as pl
from jax.experimental.pallas import tpu as pltpu
from jax.sharding import PartitionSpec as P

SOFTMAX_TEMPER = 0.5
EPSILON = 1e-05

LANES = 128
META = 16
UA = 8
UB = 16
UC = 16
CHUNK = 16
EXTRA = 4


def pack_kernel(
    assign, neighbour, features, diag, coupling, feature_drop, edge_drop, send, meta
):
    owned, nodes, columns = features.shape[1:]
    blocks = columns // LANES
    meta[...] = jnp.zeros_like(meta)
    send[:, pl.ds(0, (blocks + 2) * nodes), :] = jnp.zeros(
        (send.shape[0], (blocks + 2) * nodes, LANES), jnp.bfloat16
    )
    for k in range(owned):
        target = assign[0, k]
        for j in range(blocks):
            send[target, pl.ds(j * nodes, nodes), :] = features[0, k, :, pl.ds(j * LANES, LANES)]
        send[target, pl.ds(blocks * nodes, nodes), :] = diag[0, k]
        send[target, pl.ds((blocks + 1) * nodes, nodes), :] = coupling[0, k]
        for v in range(2):
            for j in range(blocks):
                meta[target, v * blocks + j, :] = feature_drop[
                    0, k, v, pl.ds(j * LANES, LANES)
                ].astype(jnp.float32)
            meta[target, 2 * blocks + v, :] = edge_drop[0, k, v, :].astype(jnp.float32)
        slot = neighbour[0, k] // owned + 1
        meta[target, 2 * blocks + 2, :] = jnp.full((LANES,), slot, jnp.float32)
    send[:, pl.ds((blocks + 2) * nodes, META), :] = meta[...].astype(jnp.bfloat16)


def dot(a, b, contract, precision=None):
    return lax.dot_general(
        a, b, (contract, ((), ())), precision=precision, preferred_element_type=jnp.float32
    )


def step_kernel(
    core, weights, recv, out,
    slots, links, first, extra_count, extra_to, extra_from,
    h0, p0, p1, h1, near, far, active, sums, pooled, link_sem,
):
    count = recv.shape[0]
    columns = weights.shape[1]
    blocks = columns // LANES
    nodes = near.shape[1]
    body = (blocks + 2) * nodes
    rows = 2 * nodes
    chunk = sums.shape[0] // rows
    low = jnp.bfloat16

    slots[...] = recv[:, pl.ds(body, META), :].astype(jnp.float32)
    pooled[2, :, pl.ds(0, LANES)] = slots[:, 2 * blocks + 2, :]
    found = slots[:, 2 * blocks + 2, :].astype(jnp.int32) - 1
    itself = lax.broadcasted_iota(jnp.int32, found.shape, 0)

    def put_links(staged):
        staged[...] = jnp.where(found < 0, itself, found)
        copy = pltpu.make_async_copy(staged, links, link_sem)
        copy.start()
        copy.wait()

    pl.run_scoped(put_links, pltpu.VMEM((count, LANES), jnp.int32))

    for s in range(count):
        first[s] = count
    for i in range(count // chunk):
        extra_count[i] = 0

    def enlist(s, carry):
        n = links[s, 0]
        i = n // chunk
        taken = first[n] != count

        @pl.when(taken)
        def _():
            k = extra_count[i]
            extra_to[i * count + k] = n
            extra_from[i * count + k] = s
            extra_count[i] = k + 1

        @pl.when(jnp.logical_not(taken))
        def _():
            first[n] = s

        return carry

    lax.fori_loop(0, count, enlist, 0)
    for i in range(count // chunk):
        for d in range(EXTRA - 1):
            extra_to[i * count + extra_count[i] + d] = i * chunk
            extra_from[i * count + extra_count[i] + d] = count
    far[pl.ds(2 * count, 2)] = jnp.zeros((2, nodes, nodes), low)

    def each(width, stage, then=None):
        def steps(i, carry):
            for u in range(width):
                stage(i * width + u)
            if then is not None:
                then(pl.ds(i * width * rows, width * rows))
            return carry

        lax.fori_loop(0, count // width, steps, 0)

    def part(s, v):
        return pl.ds(s * rows + v * nodes, nodes)

    def project(s):
        n = links[s, 0]
        for v in range(2):
            pieces = []
            for j in range(blocks):
                keep = slots[s, pl.ds(v * blocks + j, 1), :].astype(low)
                pieces.append(recv[s, pl.ds(j * nodes, nodes), :] * keep)
            h0[part(s, v), :] = jnp.concatenate(pieces, axis=1)
            own_keep = slots[s, pl.ds(2 * blocks + v, 1), :].astype(low)
            far_keep = slots[n, pl.ds(2 * blocks + v, 1), :].astype(low)
            near[2 * s + v] = recv[s, pl.ds(blocks * nodes, nodes), :] * own_keep
            far[2 * s + v] = recv[s, pl.ds((blocks + 1) * nodes, nodes), :] * far_keep

    def project_rows(span):
        p0[span, :] = dot(h0[span, :], weights[0], ((1,), (0,))).astype(low)

    each(UA, project, project_rows)

    def gather(source, s, v):
        n = links[s, 0]
        return dot(
            jnp.concatenate([near[2 * s + v], far[2 * s + v]], axis=1),
            jnp.concatenate([source[part(s, v), :], source[part(n, v), :]], axis=0),
            ((1,), (0,)),
        )

    def first_layer(s):
        for v in range(2):
            h1[part(s, v), :] = jnp.maximum(gather(p0, s, v), 0.0).astype(low)

    def first_rows(span):
        p1[span, :] = dot(h1[span, :], weights[1], ((1,), (0,))).astype(low)

    each(UB, first_layer, first_rows)

    def second_layer(s):
        for v in range(2):
            summed = jnp.maximum(gather(p1, s, v), 0.0)
            active[part(s, v), :] = jnp.where(summed > 0, 1.0, 0.0).astype(low)
            pooled[v, pl.ds(s, 1), :] = jnp.sum(summed, axis=0, keepdims=True) * (1.0 / nodes)

    each(UC, second_layer)

    flags = jnp.where(pooled[2, :, pl.ds(0, LANES)] > 0.5, 1.0, 0.0)
    occ_col = flags[:, 0:1]
    occ_row = dot(
        jnp.full((8, LANES), 1.0 / LANES, jnp.float32), flags, ((1,), (1,)), lax.Precision.HIGHEST
    )[0:1, :]
    means = [pooled[0], pooled[1]]
    inv = [lax.rsqrt(jnp.mean(e * e, axis=-1, keepdims=True) + EPSILON) for e in means]
    unit = [e * i for e, i in zip(means, inv)]
    scale = 1.0 / (columns * SOFTMAX_TEMPER)
    high = lax.Precision.HIGHEST
    scores = dot(unit[0], unit[1], ((1,), (1,)), high) * scale
    weighted = jnp.exp(scores) * occ_row
    totals = jnp.where(occ_col > 0.5, jnp.sum(weighted, axis=1, keepdims=True), 1.0)
    row_id = lax.broadcasted_iota(jnp.int32, (count, count), 0)
    col_id = lax.broadcasted_iota(jnp.int32, (count, count), 1)
    eye = jnp.where(row_id == col_id, 1.0, 0.0)
    coeffs = (weighted / totals - eye) * occ_col
    unit_grad = [
        dot(coeffs, unit[1], ((1,), (0,)), high) * scale,
        dot(coeffs, unit[0], ((0,), (0,)), high) * scale,
    ]
    for v in range(2):
        grad = (
            inv[v] * unit_grad[v]
            - (inv[v] ** 3 * jnp.sum(means[v] * unit_grad[v], axis=-1, keepdims=True) / columns)
            * means[v]
        )
        pooled[v] = (grad / nodes).astype(low).astype(jnp.float32)

    def spread(i, grad_of):
        for u in range(chunk):
            s = i * chunk + u
            a = first[s]
            b = jnp.minimum(a, count - 1)
            for v in range(2):
                sums[pl.ds(u * rows + v * nodes, nodes), :] = dot(
                    jnp.concatenate([near[2 * s + v], far[2 * a + v]], axis=0),
                    jnp.concatenate([grad_of(s, v), grad_of(b, v)], axis=0),
                    ((0,), (0,)),
                )

        def further(t, carry):
            parts = []
            for d in range(EXTRA):
                k = i * count + t * EXTRA + d
                a = extra_from[k]
                b = jnp.minimum(a, count - 1)
                for v in range(2):
                    mine = part(extra_to[k] - i * chunk, v)
                    parts.append((mine, dot(far[2 * a + v], grad_of(b, v), ((0,), (0,)))))
            for mine, more in parts:
                sums[mine, :] = sums[mine, :] + more
            return carry

        lax.fori_loop(0, (extra_count[i] + EXTRA - 1) // EXTRA, further, 0)
        return sums[...].astype(low)

    def second_grad(s, v):
        return active[part(s, v), :] * pooled[v, pl.ds(s, 1), :].astype(low)

    grad = spread(0, second_grad)
    out[core[0] ^ 1] = dot(h1[...], grad, ((0,), (0,)))
    below = dot(grad, weights[1], ((1,), (1,)))
    p0[...] = jnp.where(h1[...] > 0, below, 0.0).astype(low)

    def first_grad(s, v):
        return p0[part(s, v), :]

    out[core[0]] = dot(h0[...], spread(0, first_grad), ((0,), (0,)))


def local(
    features, diag_blocks, coupling_blocks, neighbour, assignment, feature_drop, edge_drop, weights
):
    count = lax.axis_size("batch")
    stores = lax.axis_size("store")
    _, owned, nodes, columns = features.shape
    blocks = columns // LANES
    body = (blocks + 2) * nodes
    low = jnp.bfloat16
    smem = pl.BlockSpec(memory_space=pltpu.SMEM)
    vmem = pl.BlockSpec(memory_space=pltpu.VMEM)
    send = pl.pallas_call(
        pack_kernel,
        out_shape=jax.ShapeDtypeStruct((count, body + META, LANES), low),
        in_specs=[smem, smem, vmem, vmem, vmem, vmem, vmem],
        out_specs=vmem,
        scratch_shapes=[pltpu.VMEM((count, META, LANES), jnp.float32)],
        name="pack",
    )(assignment, neighbour, features, diag_blocks, coupling_blocks, feature_drop, edge_drop)
    parity = lax.axis_index("store") % 2
    send, parity = lax.optimization_barrier((send, parity))
    recv = lax.all_to_all(send, "batch", split_axis=0, concat_axis=0, tiled=True)
    total = count * 2 * nodes
    halves = pl.pallas_call(
        step_kernel,
        out_shape=jax.ShapeDtypeStruct((2, columns, columns), jnp.float32),
        in_specs=[smem, vmem, vmem],
        out_specs=vmem,
        scratch_shapes=[
            pltpu.VMEM((count, META, LANES), jnp.float32),
            pltpu.SMEM((count, LANES), jnp.int32),
            pltpu.SMEM((count,), jnp.int32),
            pltpu.SMEM((count,), jnp.int32),
            pltpu.SMEM((2 * count * count,), jnp.int32),
            pltpu.SMEM((2 * count * count,), jnp.int32),
            pltpu.VMEM((total, columns), low),
            pltpu.VMEM((total, columns), low),
            pltpu.VMEM((total, columns), low),
            pltpu.VMEM((total, columns), low),
            pltpu.VMEM((2 * count, nodes, nodes), low),
            pltpu.VMEM((2 * count + 2, nodes, nodes), low),
            pltpu.VMEM((total, columns), low),
            pltpu.VMEM((CHUNK * 2 * nodes, columns), jnp.float32),
            pltpu.VMEM((3, count, columns), jnp.float32),
            pltpu.SemaphoreType.DMA,
        ],
        compiler_params=pltpu.CompilerParams(vmem_limit_bytes=46 << 20),
        name="step",
    )(parity.reshape(1).astype(jnp.int32), weights, recv)

    swap = [(s, s ^ 1) for s in range(stores)]
    kept = halves[0] + lax.ppermute(halves[1], "store", swap)
    chips = stores // 2 * count
    groups = [
        [s * count + b for s in range(c, stores, 2) for b in range(count)] for c in range(2)
    ]
    axes = ("store", "batch")
    pieces = lax.all_to_all(
        kept.reshape(chips, columns // chips, columns),
        axes, split_axis=0, concat_axis=0, axis_index_groups=groups, tiled=True,
    )
    piece = jnp.sum(pieces, axis=0).astype(low)
    layer = lax.all_to_all(
        jnp.broadcast_to(piece[None], (chips,) + piece.shape),
        axes, split_axis=0, concat_axis=0, axis_index_groups=groups, tiled=True,
    ).reshape(columns, columns)
    other = lax.ppermute(layer, "store", swap)
    first = parity == 0
    return jnp.stack(
        [jnp.where(first, layer, other), jnp.where(first, other, layer)]
    ).astype(jnp.float32)


def solution(mesh):
    return jax.shard_map(
        local,
        mesh=mesh,
        in_specs=(
            P("store", "batch", None, None),
            P("store", "batch", None, None),
            P("store", "batch", None, None),
            P("store", "batch"),
            P("store", "batch"),
            P("store", "batch", None, None),
            P("store", "batch", None, None),
            P(),
        ),
        out_specs=P(),
        check_vma=False,
    )
```

```python
import jax
import jax.numpy as jnp
from jax import lax
from jax.experimental import pallas as pl
from jax.experimental.pallas import tpu as pltpu
from jax.sharding import PartitionSpec as P

SOFTMAX_TEMPER = 0.5
EPSILON = 1e-05

LANES = 128
META = 16
UA = 8
UB = 16
UC = 16
CHUNK = 16
EXTRA = 4


def pack_kernel(
    assign, neighbour, features, diag, coupling, feature_drop, edge_drop, send,
    targets, links, used, rows, kept_features, kept_edges, meta, staged, sems, block_sems, out_sems,
):
    owned, nodes, columns = features.shape[1:]
    count = send.shape[0]
    blocks = columns // LANES
    loads = [
        pltpu.make_async_copy(source, place, sems.at[i])
        for i, (source, place) in enumerate(
            [
                (assign, targets),
                (neighbour, links),
                (feature_drop, kept_features),
                (edge_drop, kept_edges),
            ]
        )
    ]
    loads += [
        pltpu.make_async_copy(features.at[0, k], rows.at[k], sems.at[4 + k]) for k in range(owned)
    ]
    for load in loads:
        load.start()
    meta[...] = jnp.zeros_like(meta)
    for s in range(count):
        used[s] = 0
    loads[0].wait()
    block_loads = []
    for k in range(owned):
        target = targets[0, k]
        used[target] = 1
        for i, source in enumerate((diag, coupling)):
            load = pltpu.make_async_copy(
                source.at[0, k],
                staged.at[target, pl.ds((blocks + i) * nodes, nodes), :],
                block_sems.at[k, i],
            )
            load.start()
            block_loads.append(load)
    for load in loads[1:4]:
        load.wait()
    for k in range(owned):
        target = targets[0, k]
        for v in range(2):
            for j in range(blocks):
                meta[target, v * blocks + j, :] = kept_features[
                    0, k, v, pl.ds(j * LANES, LANES)
                ].astype(jnp.float32)
            meta[target, 2 * blocks + v, :] = kept_edges[0, k, v, :].astype(jnp.float32)
        slot = links[0, k] // owned + 1
        meta[target, 2 * blocks + 2, :] = jnp.full((LANES,), slot, jnp.float32)
    staged[:, pl.ds((blocks + 2) * nodes, META), :] = meta[...].astype(jnp.bfloat16)

    def leave(s):
        return pltpu.make_async_copy(staged.at[s], send.at[s], out_sems.at[s])

    for s in range(count):

        @pl.when(used[s] == 0)
        def _():
            staged[s] = jnp.zeros(staged.shape[1:], jnp.bfloat16)
            leave(s).start()

    for k in range(owned):
        target = targets[0, k]
        loads[4 + k].wait()
        for j in range(blocks):
            staged[target, pl.ds(j * nodes, nodes), :] = rows[k, :, pl.ds(j * LANES, LANES)]
        block_loads[2 * k].wait()
        block_loads[2 * k + 1].wait()
        leave(target).start()
    for s in range(count):
        leave(s).wait()


def dot(a, b, contract, precision=None):
    return lax.dot_general(
        a, b, (contract, ((), ())), precision=precision, preferred_element_type=jnp.float32
    )


def step_kernel(
    core, weights, recv, out,
    slots, links, first, extra_count, extra_to, extra_from,
    h0, p0, p1, h1, near, far, active, sums, pooled, link_sem,
):
    count = recv.shape[0]
    columns = weights.shape[1]
    blocks = columns // LANES
    nodes = near.shape[1]
    body = (blocks + 2) * nodes
    rows = 2 * nodes
    chunk = sums.shape[0] // rows
    low = jnp.bfloat16

    slots[...] = recv[:, pl.ds(body, META), :].astype(jnp.float32)
    pooled[2, :, pl.ds(0, LANES)] = slots[:, 2 * blocks + 2, :]
    found = slots[:, 2 * blocks + 2, :].astype(jnp.int32) - 1
    itself = lax.broadcasted_iota(jnp.int32, found.shape, 0)

    def put_links(staged):
        staged[...] = jnp.where(found < 0, itself, found)
        copy = pltpu.make_async_copy(staged, links, link_sem)
        copy.start()
        copy.wait()

    pl.run_scoped(put_links, pltpu.VMEM((count, LANES), jnp.int32))

    for s in range(count):
        first[s] = count
    for i in range(count // chunk):
        extra_count[i] = 0

    def enlist(s, carry):
        n = links[s, 0]
        i = n // chunk
        taken = first[n] != count

        @pl.when(taken)
        def _():
            k = extra_count[i]
            extra_to[i * count + k] = n
            extra_from[i * count + k] = s
            extra_count[i] = k + 1

        @pl.when(jnp.logical_not(taken))
        def _():
            first[n] = s

        return carry

    lax.fori_loop(0, count, enlist, 0)
    for i in range(count // chunk):
        for d in range(EXTRA - 1):
            extra_to[i * count + extra_count[i] + d] = i * chunk
            extra_from[i * count + extra_count[i] + d] = count
    far[pl.ds(2 * count, 2)] = jnp.zeros((2, nodes, nodes), low)

    def each(width, stage, then=None):
        def steps(i, carry):
            for u in range(width):
                stage(i * width + u)
            if then is not None:
                then(pl.ds(i * width * rows, width * rows))
            return carry

        lax.fori_loop(0, count // width, steps, 0)

    def part(s, v):
        return pl.ds(s * rows + v * nodes, nodes)

    def project(s):
        n = links[s, 0]
        for v in range(2):
            pieces = []
            for j in range(blocks):
                keep = slots[s, pl.ds(v * blocks + j, 1), :].astype(low)
                pieces.append(recv[s, pl.ds(j * nodes, nodes), :] * keep)
            h0[part(s, v), :] = jnp.concatenate(pieces, axis=1)
            own_keep = slots[s, pl.ds(2 * blocks + v, 1), :].astype(low)
            far_keep = slots[n, pl.ds(2 * blocks + v, 1), :].astype(low)
            near[2 * s + v] = recv[s, pl.ds(blocks * nodes, nodes), :] * own_keep
            far[2 * s + v] = recv[s, pl.ds((blocks + 1) * nodes, nodes), :] * far_keep

    def project_rows(span):
        p0[span, :] = dot(h0[span, :], weights[0], ((1,), (0,))).astype(low)

    each(UA, project, project_rows)

    def gather(source, s, v):
        n = links[s, 0]
        return dot(
            jnp.concatenate([near[2 * s + v], far[2 * s + v]], axis=1),
            jnp.concatenate([source[part(s, v), :], source[part(n, v), :]], axis=0),
            ((1,), (0,)),
        )

    def first_layer(s):
        for v in range(2):
            h1[part(s, v), :] = jnp.maximum(gather(p0, s, v), 0.0).astype(low)

    def first_rows(span):
        p1[span, :] = dot(h1[span, :], weights[1], ((1,), (0,))).astype(low)

    each(UB, first_layer, first_rows)

    def second_layer(s):
        for v in range(2):
            summed = jnp.maximum(gather(p1, s, v), 0.0)
            active[part(s, v), :] = jnp.where(summed > 0, 1.0, 0.0).astype(low)
            pooled[v, pl.ds(s, 1), :] = jnp.sum(summed, axis=0, keepdims=True) * (1.0 / nodes)

    each(UC, second_layer)

    flags = jnp.where(pooled[2, :, pl.ds(0, LANES)] > 0.5, 1.0, 0.0)
    occ_col = flags[:, 0:1]
    occ_row = dot(
        jnp.full((8, LANES), 1.0 / LANES, jnp.float32), flags, ((1,), (1,)), lax.Precision.HIGHEST
    )[0:1, :]
    means = [pooled[0], pooled[1]]
    inv = [lax.rsqrt(jnp.mean(e * e, axis=-1, keepdims=True) + EPSILON) for e in means]
    unit = [e * i for e, i in zip(means, inv)]
    scale = 1.0 / (columns * SOFTMAX_TEMPER)
    high = lax.Precision.HIGHEST
    scores = dot(unit[0], unit[1], ((1,), (1,)), high) * scale
    weighted = jnp.exp(scores) * occ_row
    totals = jnp.where(occ_col > 0.5, jnp.sum(weighted, axis=1, keepdims=True), 1.0)
    row_id = lax.broadcasted_iota(jnp.int32, (count, count), 0)
    col_id = lax.broadcasted_iota(jnp.int32, (count, count), 1)
    eye = jnp.where(row_id == col_id, 1.0, 0.0)
    coeffs = (weighted / totals - eye) * occ_col
    unit_grad = [
        dot(coeffs, unit[1], ((1,), (0,)), high) * scale,
        dot(coeffs, unit[0], ((0,), (0,)), high) * scale,
    ]
    for v in range(2):
        grad = (
            inv[v] * unit_grad[v]
            - (inv[v] ** 3 * jnp.sum(means[v] * unit_grad[v], axis=-1, keepdims=True) / columns)
            * means[v]
        )
        pooled[v] = (grad / nodes).astype(low).astype(jnp.float32)

    def spread(i, grad_of):
        for u in range(chunk):
            s = i * chunk + u
            a = first[s]
            b = jnp.minimum(a, count - 1)
            for v in range(2):
                sums[pl.ds(u * rows + v * nodes, nodes), :] = dot(
                    jnp.concatenate([near[2 * s + v], far[2 * a + v]], axis=0),
                    jnp.concatenate([grad_of(s, v), grad_of(b, v)], axis=0),
                    ((0,), (0,)),
                )

        def further(t, carry):
            parts = []
            for d in range(EXTRA):
                k = i * count + t * EXTRA + d
                a = extra_from[k]
                b = jnp.minimum(a, count - 1)
                for v in range(2):
                    mine = part(extra_to[k] - i * chunk, v)
                    parts.append((mine, dot(far[2 * a + v], grad_of(b, v), ((0,), (0,)))))
            for mine, more in parts:
                sums[mine, :] = sums[mine, :] + more
            return carry

        lax.fori_loop(0, (extra_count[i] + EXTRA - 1) // EXTRA, further, 0)
        return sums[...].astype(low)

    def second_grad(s, v):
        return active[part(s, v), :] * pooled[v, pl.ds(s, 1), :].astype(low)

    grad = spread(0, second_grad)
    out[core[0] ^ 1] = dot(h1[...], grad, ((0,), (0,)))
    below = dot(grad, weights[1], ((1,), (1,)))
    p0[...] = jnp.where(h1[...] > 0, below, 0.0).astype(low)

    def first_grad(s, v):
        return p0[part(s, v), :]

    out[core[0]] = dot(h0[...], spread(0, first_grad), ((0,), (0,)))


def local(
    features, diag_blocks, coupling_blocks, neighbour, assignment, feature_drop, edge_drop, weights
):
    count = lax.axis_size("batch")
    stores = lax.axis_size("store")
    _, owned, nodes, columns = features.shape
    blocks = columns // LANES
    body = (blocks + 2) * nodes
    low = jnp.bfloat16
    smem = pl.BlockSpec(memory_space=pltpu.SMEM)
    vmem = pl.BlockSpec(memory_space=pltpu.VMEM)
    raw = pl.BlockSpec(memory_space=pl.ANY)
    send = pl.pallas_call(
        pack_kernel,
        out_shape=jax.ShapeDtypeStruct((count, body + META, LANES), low),
        in_specs=[raw] * 7,
        out_specs=raw,
        scratch_shapes=[
            pltpu.SMEM((1, owned), jnp.int32),
            pltpu.SMEM((1, owned), jnp.int32),
            pltpu.SMEM((count,), jnp.int32),
            pltpu.VMEM((owned, nodes, columns), low),
            pltpu.VMEM(feature_drop.shape, jnp.int32),
            pltpu.VMEM(edge_drop.shape, jnp.int32),
            pltpu.VMEM((count, META, LANES), jnp.float32),
            pltpu.VMEM((count, body + META, LANES), low),
            pltpu.SemaphoreType.DMA((4 + owned,)),
            pltpu.SemaphoreType.DMA((owned, 2)),
            pltpu.SemaphoreType.DMA((count,)),
        ],
        name="pack",
    )(assignment, neighbour, features, diag_blocks, coupling_blocks, feature_drop, edge_drop)
    parity = lax.axis_index("store") % 2
    send, parity = lax.optimization_barrier((send, parity))
    recv = lax.all_to_all(send, "batch", split_axis=0, concat_axis=0, tiled=True)
    total = count * 2 * nodes
    halves = pl.pallas_call(
        step_kernel,
        out_shape=jax.ShapeDtypeStruct((2, columns, columns), jnp.float32),
        in_specs=[smem, vmem, vmem],
        out_specs=vmem,
        scratch_shapes=[
            pltpu.VMEM((count, META, LANES), jnp.float32),
            pltpu.SMEM((count, LANES), jnp.int32),
            pltpu.SMEM((count,), jnp.int32),
            pltpu.SMEM((count,), jnp.int32),
            pltpu.SMEM((2 * count * count,), jnp.int32),
            pltpu.SMEM((2 * count * count,), jnp.int32),
            pltpu.VMEM((total, columns), low),
            pltpu.VMEM((total, columns), low),
            pltpu.VMEM((total, columns), low),
            pltpu.VMEM((total, columns), low),
            pltpu.VMEM((2 * count, nodes, nodes), low),
            pltpu.VMEM((2 * count + 2, nodes, nodes), low),
            pltpu.VMEM((total, columns), low),
            pltpu.VMEM((CHUNK * 2 * nodes, columns), jnp.float32),
            pltpu.VMEM((3, count, columns), jnp.float32),
            pltpu.SemaphoreType.DMA,
        ],
        compiler_params=pltpu.CompilerParams(vmem_limit_bytes=46 << 20),
        name="step",
    )(parity.reshape(1).astype(jnp.int32), weights, recv)

    swap = [(s, s ^ 1) for s in range(stores)]
    kept = halves[0] + lax.ppermute(halves[1], "store", swap)
    chips = stores // 2 * count
    groups = [
        [s * count + b for s in range(c, stores, 2) for b in range(count)] for c in range(2)
    ]
    axes = ("store", "batch")
    pieces = lax.all_to_all(
        kept.reshape(chips, columns // chips, columns),
        axes, split_axis=0, concat_axis=0, axis_index_groups=groups, tiled=True,
    )
    piece = jnp.sum(pieces, axis=0).astype(low)
    layer = lax.all_to_all(
        jnp.broadcast_to(piece[None], (chips,) + piece.shape),
        axes, split_axis=0, concat_axis=0, axis_index_groups=groups, tiled=True,
    ).reshape(columns, columns)
    other = lax.ppermute(layer, "store", swap)
    first = parity == 0
    return jnp.stack(
        [jnp.where(first, layer, other), jnp.where(first, other, layer)]
    ).astype(jnp.float32)


def solution(mesh):
    return jax.shard_map(
        local,
        mesh=mesh,
        in_specs=(
            P("store", "batch", None, None),
            P("store", "batch", None, None),
            P("store", "batch", None, None),
            P("store", "batch"),
            P("store", "batch"),
            P("store", "batch", None, None),
            P("store", "batch", None, None),
            P(),
        ),
        out_specs=P(),
        check_vma=False,
    )
```
